256 devices in a mesh: box: 2 (over x_hi), dir: 128 (over z, y, x_lo, core).
Axes of the slice: x: 4 (x_hi: 2, x_lo: 2; x = x_hi * 2 + x_lo), y: 4, z: 8, core: 2. Of those that a mesh axis runs over, the one named last changes fastest.
Arguments:
- leaf_patterns: bfloat16 [4096, 2, 8, 1024], P(('box', 'dir')), may hold values from -6 to 6
- octant: int32 [4096], P(('box', 'dir')), may hold values from 0 to 7, as said below
- interp: bfloat16 [1024, 4096], replicated, may hold values from -0.1875 to 0.1875
- shift_angle: float32 [8, 4096], replicated, may hold values from -3.140625 to 3.140625
- partners: int32 [512, 27], P('box'), may hold values from 0 to 511, as said below
- types: int32 [512, 27], P('box'), may hold values from 0 to 342, as said below
- translators: float32 [343, 2, 4096], P(None, None, 'dir'), may hold values from -1 to 1
Outputs:
- leaf_incoming: bfloat16 [4096, 2, 8, 1024], P(('box', 'dir'))
The draws below stay inside these ranges and needn't reach their ends.
Inputs may be any that keep to these rules, and one draw needn't show every extreme that they name: The leaf boxes 8 p to 8 p + 7 are the children of parent box p; octant gives each child its position in the parent, each of 0 to 7 once among the 8 children. Parent boxes form a grid indexed in Morton order (bit j of the index is a bit of coordinate j % 3). The 27 partners of a box are distinct boxes within three boxes of it along every dimension, and none is the box itself or one of its 26 neighbours. types[p, k] = 49 (dx + 3) + 7 (dy + 3) + (dz + 3), where (dx, dy, dz) is the grid offset from box p to partners[p, k].
All inputs are finite; a program needn't handle non-finite values.
Results may differ from the reference program's by a relative error of at most 0.0064.
Values may be sent and summed in bfloat16 or wider, within the bound.
A program may use at most 64 MiB of HBM per device.

```python
import jax
import jax.numpy as jnp
from jax import lax

NDIR_L = 1024
NDIR_P = 4096
EXC = 8
OFFSETS = 343
NB_L = 4096
NB_P = 512


def geometry(key):
    levels = NB_P.bit_length() - 1
    index = jnp.arange(NB_P, dtype=jnp.int32)
    coords = [jnp.zeros((NB_P,), jnp.int32) for axis_id in range(3)]
    extent = [1, 1, 1]
    for bit in range(levels):
        axis_id = bit % 3
        coords[axis_id] = coords[axis_id] + index // 2 ** bit % 2 * 2 ** (bit // 3)
        extent[axis_id] = extent[axis_id] * 2
    offset = jnp.arange(343, dtype=jnp.int32)
    deltas = [offset // 49 - 3, offset // 7 % 7 - 3, offset % 7 - 3]
    inside = jnp.ones((NB_P, 343), dtype=bool)
    target_coords = []
    for axis_id in range(3):
        moved = coords[axis_id][:, None] + deltas[axis_id][None, :]
        inside = inside & (moved >= 0) & (moved < extent[axis_id])
        target_coords.append(jnp.clip(moved, 0, extent[axis_id] - 1))
    reach = jnp.maximum(jnp.maximum(jnp.abs(deltas[0]), jnp.abs(deltas[1])), jnp.abs(deltas[2]))
    valid = inside & (reach >= 2)[None, :]
    target = jnp.zeros((NB_P, 343), jnp.int32)
    for bit in range(levels):
        axis_id = bit % 3
        target = target + target_coords[axis_id] // 2 ** (bit // 3) % 2 * 2 ** bit
    scores = jax.random.randint(jax.random.fold_in(key, 7), (NB_P, 343), 0, 65536) * 343 + offset[None, :]
    scores = jnp.where(valid, scores, -1)
    chosen = lax.top_k(scores, 27)[1].astype(jnp.int32)
    linked = jnp.take_along_axis(target, chosen, axis=1).astype(jnp.int32)
    return (linked, chosen)


def draw_partners(key, part):
    return geometry(key)[0]


def draw_types(key, part):
    return geometry(key)[1]


def draw_octant(key, part):
    groups = NB_L // 8
    scores = jax.random.randint(jax.random.fold_in(key, 3), (groups, 8), 0, 65536) * 8 + jnp.arange(8, dtype=jnp.int32)[None, :]
    order = jnp.argsort(scores, axis=1, stable=True)
    return order.reshape(-1).astype(jnp.int32)


def level_of(key, dims, split, least, top_value):
    factor_of = 1.0
    for axis_at, parts in split:
        steps = jax.random.uniform(jax.random.fold_in(jax.random.fold_in(key, 6), axis_at), (parts,), jnp.float32, least / len(split), top_value / len(split))
        factor_of = factor_of * jnp.repeat(jnp.exp(steps), dims[axis_at] // parts).reshape((-1,) + (1,) * (len(dims) - 1 - axis_at))
    return factor_of


def scatter_about(stream_key, shape, width, limit, shards=(), kind=jnp.bfloat16):
    array = width * jax.random.normal(stream_key, shape, jnp.float32)
    if shards:
        array = array * level_of(stream_key, shape, shards, -0.22, 0.18)
    return jnp.clip(array, -limit, limit).astype(kind)


def setup_inputs(seed: int = 0) -> dict:
    key_of = jax.random.split(jax.random.key(seed), 8)
    return {
        "leaf_patterns": scatter_about(key_of[0], (NB_L, 2, EXC, NDIR_L), 1.0, 6.0, ((0, 256),)),
        "octant": draw_octant(jax.random.fold_in(key_of[7], 71), 0),
        "interp": scatter_about(key_of[2], (NDIR_L, NDIR_P), NDIR_L ** -0.5, 0.1875),
        "shift_angle": jnp.clip(jax.random.uniform(key_of[3], (8, NDIR_P), jnp.float32, -3.140625, 3.140625), -3.140625, 3.140625),
        "partners": draw_partners(jax.random.fold_in(key_of[7], 71), 0),
        "types": draw_types(jax.random.fold_in(key_of[7], 71), 0),
        "translators": scatter_about(key_of[6], (OFFSETS, 2, NDIR_P), 0.15, 1.0, ((2, 128),), jnp.float32),
    }


def reference(leaf_patterns, octant, interp, shift_angle, partners, types, translators):
    cosines = jnp.cos(shift_angle)
    sines = jnp.sin(shift_angle)
    boxes, pairs, excite, low = leaf_patterns.shape
    high = interp.shape[1]
    parents = boxes // 8
    block = min(64, parents)
    count = parents // block

    def lift(item):
        leaf_block, octant_block = item
        up = jnp.dot(leaf_block.reshape(-1, low), interp, preferred_element_type=jnp.float32)
        up = up.reshape(block * 8, 2, excite, high)
        cos_child = cosines[octant_block][:, None, :]
        sin_child = sines[octant_block][:, None, :]
        real = up[:, 0] * cos_child - up[:, 1] * sin_child
        imag = up[:, 0] * sin_child + up[:, 1] * cos_child
        summed = jnp.stack([real, imag], 1).reshape(block, 8, 2, excite, high).sum(axis=1)
        return summed.astype(jnp.bfloat16)

    aggregated = lax.map(lift, (leaf_patterns.reshape(count, block * 8, 2, excite, low),
                                octant.reshape(count, block * 8)))
    aggregated = aggregated.reshape(parents, 2, excite, high)

    def translate(step, total):
        source = jnp.take(aggregated, partners[:, step], axis=0).astype(jnp.float32)
        factor = jnp.take(translators, types[:, step], axis=0)
        factor_re = factor[:, 0][:, None, :]
        factor_im = factor[:, 1][:, None, :]
        real = factor_re * source[:, 0] - factor_im * source[:, 1]
        imag = factor_re * source[:, 1] + factor_im * source[:, 0]
        return total + jnp.stack([real, imag], 1)

    zero = jnp.zeros((parents, 2, excite, high), jnp.float32)
    incoming = lax.fori_loop(0, partners.shape[1], translate, zero).astype(jnp.bfloat16)
    scale = low / high

    def descend(item):
        parent_block, octant_block = item
        spread = jnp.repeat(parent_block.astype(jnp.float32), 8, axis=0)
        cos_child = cosines[octant_block][:, None, :]
        sin_child = sines[octant_block][:, None, :]
        real = spread[:, 0] * cos_child + spread[:, 1] * sin_child
        imag = spread[:, 1] * cos_child - spread[:, 0] * sin_child
        shifted = jnp.stack([real, imag], 1).astype(jnp.bfloat16).reshape(-1, high)
        down = lax.dot_general(shifted, interp, (((1,), (1,)), ((), ())), preferred_element_type=jnp.float32)
        return (down * scale).astype(jnp.bfloat16).reshape(block * 8, 2, excite, low)

    leaf_incoming = lax.map(descend, (incoming.reshape(count, block, 2, excite, high),
                                      octant.reshape(count, block * 8)))
    return leaf_incoming.reshape(boxes, 2, excite, low)
```

```python
import jax
import jax.numpy as jnp
from jax import lax
from jax.experimental import pallas as pl
from jax.experimental.pallas import tpu as pltpu
from jax.sharding import PartitionSpec as P

MESH = pl.DeviceIdType.MESH
Z = 8
PLANE = 32
WIDTH = 16
CHUNK = PLANE * WIDTH
PB = 64
LINKED = 27
ROWS = PB * LINKED
BLOCKS = Z * 2 * PLANE // PB
TYPES = 384
F32, BF16 = jnp.float32, jnp.bfloat16


def block_transpose(xs):
    block = lax.broadcasted_iota(jnp.int32, xs[0].shape, 1) // 16
    for step in (1, 2, 4):
        low = (block // step) % 2 == 0
        out = list(xs)
        for i in range(8):
            if i & step == 0:
                a, b = xs[i], xs[i + step]
                out[i] = jnp.where(low, a, pltpu.roll(b, 16 * step, 1))
                out[i + step] = jnp.where(low, pltpu.roll(a, 128 - 16 * step, 1), b)
        xs = out
    return xs


def kernel(
    oct_ref, leaf_ref, interp_ref, cos_ref, sin_ref, idx_ref, tr_ref, out_ref,
    interp_v, zsend, zrecv, ysend, arecv, idxall, oht, oh, fac, rsend, rrecv, xp, wsend, wrecv, shifted, acc,
    isem, zs, zr, ys, yr, xs_sem, xr_sem, rs, rr, ws, wr,
):
    box = lax.axis_index("box")
    d = lax.axis_index("dir")
    z = d // 16
    yxc = d % 16
    slab = box * 16 + yxc
    spot = yxc * 2 + box

    def plane_of_slab(s):
        return (s // 16, z * 16 + s % 16)

    def plane_of_spot(t):
        return (t % 2, z * 16 + t // 2)

    def order(i):
        half = (i + 1) // 2
        return (z + 4 + half * (1 - 2 * (i % 2))) % 8

    def fetch(i):
        zc = order(i)
        at = pl.multiple_of(zc * CHUNK, CHUNK)
        return pltpu.make_async_copy(interp_ref.at[:, pl.ds(at, CHUNK)], interp_v.at[zc], isem.at[i])

    for i in range(Z):
        fetch(i).start()

    barrier = pltpu.get_barrier_semaphore()

    def greet_z(i, carry):
        pl.semaphore_signal(barrier, inc=1, device_id=(box, (z + i) % 8 * 16 + yxc), device_id_type=MESH)
        return carry

    def greet_plane(i, carry):
        pl.semaphore_signal(barrier, inc=1, device_id=plane_of_slab((slab + i) % PLANE), device_id_type=MESH)
        return carry

    lax.fori_loop(1, Z, greet_z, 0)
    lax.fori_loop(1, PLANE, greet_plane, 0)
    pl.semaphore_wait(barrier, Z - 1 + PLANE - 1)

    idx_copy = pltpu.make_async_remote_copy(
        src_ref=idx_ref, dst_ref=idxall.at[box], send_sem=xs_sem, recv_sem=xr_sem,
        device_id=(1 - box, d), device_id_type=MESH,
    )
    idx_copy.start()

    def z_copy(src, dst, ssem, rsem, zc):
        return pltpu.make_async_remote_copy(
            src_ref=src.at[zc], dst_ref=dst.at[z], send_sem=ssem.at[zc], recv_sem=rsem.at[z],
            device_id=(box, zc * 16 + yxc), device_id_type=MESH,
        )

    def z_arrival(src, dst, ssem, rsem, zc):
        return pltpu.make_async_remote_copy(
            src_ref=src.at[zc], dst_ref=dst.at[zc], send_sem=ssem.at[zc], recv_sem=rsem.at[zc],
            device_id=(box, zc * 16 + yxc), device_id_type=MESH,
        )

    def phases(child, zc):
        o = oct_ref[child]
        at = pl.ds(pl.multiple_of(zc * CHUNK, CHUNK), CHUNK)
        return cos_ref[pl.ds(o, 1), at], sin_ref[pl.ds(o, 1), at]

    def lift(i, carry):
        zc = order(i)
        fetch(i).wait()
        up = jnp.dot(leaf_ref[...], interp_v[zc], preferred_element_type=F32)
        parts = []
        for parent in range(2):
            real = imag = None
            for k in range(8):
                child = parent * 8 + k
                cs, sn = phases(child, zc)
                ur, ui = up[child * 16 : child * 16 + 8], up[child * 16 + 8 : child * 16 + 16]
                a, b = ur * cs - ui * sn, ur * sn + ui * cs
                real, imag = (a, b) if real is None else (real + a, imag + b)
            parts += [real, imag]
        zsend[zc] = jnp.concatenate(parts, axis=0).astype(BF16)

        @pl.when(i < Z - 1)
        def _():
            z_copy(zsend, zrecv, zs, zr, zc).start()

        return carry

    lax.fori_loop(0, Z, lift, 0)
    zrecv[z] = zsend[z]

    idxall[box] = idx_ref[...]
    spread = (
        lax.broadcasted_iota(jnp.int32, (64, 256), 0)
        == lax.broadcasted_iota(jnp.int32, (64, 256), 1) // 128 * 32
        + box * WIDTH
        + lax.broadcasted_iota(jnp.int32, (64, 256), 1) % WIDTH
    )
    table = jnp.dot(tr_ref[...], spread.astype(F32).astype(BF16), preferred_element_type=F32).astype(BF16)
    idx_copy.wait()

    def indices(pb):
        half = BLOCKS // 2
        return idxall[pb // half, pl.ds(pl.multiple_of(pb % half * PB, PB), PB), :]

    def factors(pb, carry):
        index = indices(pb)
        wide = lax.broadcasted_iota(jnp.int32, (PB, TYPES), 1)
        for k in range(LINKED):
            oht[k * PB : (k + 1) * PB, :] = (wide == index[:, 32 + k : 33 + k]).astype(F32).astype(BF16)
        fac[pb] = jnp.dot(oht[...], table, preferred_element_type=F32)
        return carry

    lax.fori_loop(0, BLOCKS, factors, 0)

    def z_wait(i, carry):
        zc = (z + i) % 8
        z_arrival(zsend, zrecv, zs, zr, zc).wait_recv()
        return carry

    lax.fori_loop(1, Z, z_wait, 0)

    r0 = lax.broadcasted_iota(jnp.int32, (256, 256), 0)
    r1 = lax.broadcasted_iota(jnp.int32, (256, 256), 1)
    turn = (r1 == r0 % 16 * 16 + r0 // 16).astype(F32).astype(BF16)
    turned = jnp.dot(turn, zrecv[...].reshape(256, CHUNK), preferred_element_type=F32)
    for pair in range(2):
        for dh in range(4):
            lanes = slice(dh * 128, dh * 128 + 128)
            blocks = [turned[(pair * 8 + j) * 16 : (pair * 8 + j) * 16 + 16, lanes] for j in range(8)]
            for j, y in enumerate(block_transpose(blocks)):
                ysend[dh * 8 + j, :, pair * 128 : pair * 128 + 128] = y.astype(BF16)

    def y_copy(t):
        return pltpu.make_async_remote_copy(
            src_ref=ysend.at[t], dst_ref=arecv.at[slab], send_sem=ys.at[t], recv_sem=yr.at[slab],
            device_id=plane_of_spot(t), device_id_type=MESH,
        )

    def y_arrival(s):
        return pltpu.make_async_remote_copy(
            src_ref=ysend.at[s], dst_ref=arecv.at[s], send_sem=ys.at[s], recv_sem=yr.at[s],
            device_id=plane_of_slab(s), device_id_type=MESH,
        )

    def y_start(i, carry):
        y_copy((spot + i) % PLANE).start()
        return carry

    lax.fori_loop(1, PLANE, y_start, 0)
    arecv[slab] = ysend[spot]

    def sources(pb, carry):
        index = indices(pb)
        wide = lax.broadcasted_iota(jnp.int32, (PB, 512), 1)
        for k in range(LINKED):
            oh[pb, k * PB : (k + 1) * PB, :] = (wide == index[:, k : k + 1]).astype(F32).astype(BF16)
        return carry

    lax.fori_loop(0, BLOCKS, sources, 0)

    def y_wait(i, carry):
        y_arrival((slab + i) % PLANE).wait_recv()
        return carry

    lax.fori_loop(1, PLANE, y_wait, 0)

    def r_copy(s):
        return pltpu.make_async_remote_copy(
            src_ref=rsend.at[s], dst_ref=rrecv.at[spot], send_sem=rs.at[s], recv_sem=rr.at[spot],
            device_id=plane_of_slab(s), device_id_type=MESH,
        )

    def r_arrival(t):
        return pltpu.make_async_remote_copy(
            src_ref=rsend.at[t], dst_ref=rrecv.at[t], send_sem=rs.at[t], recv_sem=rr.at[t],
            device_id=plane_of_spot(t), device_id_type=MESH,
        )

    def translate(pb, carry):
        got = jnp.dot(oh[pb], arecv[...].reshape(512, 256), preferred_element_type=F32)
        real = imag = None
        for k in range(LINKED):
            rows = slice(k * PB, (k + 1) * PB)
            fr, fi = fac[pb, rows, 0:128], fac[pb, rows, 128:256]
            sr, si = got[rows, 0:128], got[rows, 128:256]
            a, b = fr * sr - fi * si, fr * si + fi * sr
            real, imag = (a, b) if real is None else (real + a, imag + b)
        each = jnp.concatenate([real, imag], axis=1).astype(BF16)
        for j in range(PB // 16):
            s = pb * (PB // 16) + j
            rsend[s] = each[j * 16 : j * 16 + 16]

            @pl.when(s != slab)
            def _():
                r_copy(s).start()

        return carry

    lax.fori_loop(0, BLOCKS, translate, 0)
    rrecv[spot] = rsend[slab]

    def r_wait(i, carry):
        r_arrival((spot + i) % PLANE).wait_recv()
        return carry

    lax.fori_loop(1, PLANE, r_wait, 0)

    for pair in range(2):
        for dh in range(4):
            lanes = slice(dh * 128, dh * 128 + 128)
            blocks = [rrecv[dh * 8 + j, :, pair * 128 : pair * 128 + 128].astype(F32) for j in range(8)]
            for j, y in enumerate(block_transpose(blocks)):
                xp[(pair * 8 + j) * 16 : (pair * 8 + j) * 16 + 16, lanes] = y.astype(BF16)
    wsend[...] = jnp.dot(turn, xp[...], preferred_element_type=F32).astype(BF16).reshape(Z, 32, CHUNK)

    def w_start(i, carry):
        z_copy(wsend, wrecv, ws, wr, order(i)).start()
        return carry

    lax.fori_loop(0, Z - 1, w_start, 0)
    wrecv[z] = wsend[z]
    acc[...] = jnp.zeros_like(acc)

    def descend(i, carry):
        zc = order(Z - 1 - i)

        @pl.when(i > 0)
        def _():
            z_arrival(wsend, wrecv, ws, wr, zc).wait_recv()

        got = wrecv[zc].astype(F32)
        for parent in range(2):
            re, im = got[parent * 16 : parent * 16 + 8], got[parent * 16 + 8 : parent * 16 + 16]
            for k in range(8):
                child = parent * 8 + k
                cs, sn = phases(child, zc)
                both = jnp.concatenate([re * cs + im * sn, im * cs - re * sn], axis=0)
                shifted[child * 16 : child * 16 + 16, :] = both.astype(BF16)
        acc[...] += lax.dot_general(
            shifted[...], interp_v[zc], (((1,), (1,)), ((), ())), preferred_element_type=F32
        )
        return carry

    lax.fori_loop(0, Z, descend, 0)
    out_ref[...] = (acc[...] * 0.25).astype(BF16)

    def z_sent(i, carry):
        zc = (z + i) % 8
        z_copy(zsend, zrecv, zs, zr, zc).wait_send()
        z_copy(wsend, wrecv, ws, wr, zc).wait_send()
        return carry

    def plane_sent(i, carry):
        y_copy((spot + i) % PLANE).wait_send()
        r_copy((slab + i) % PLANE).wait_send()
        return carry

    lax.fori_loop(1, Z, z_sent, 0)
    lax.fori_loop(1, PLANE, plane_sent, 0)


def local(leaf_patterns, octant, interp, shift_angle, partners, types, translators):
    boxes, pairs, excite, low = leaf_patterns.shape
    high = interp.shape[1]
    own = partners.shape[0]
    place = (partners // 256 * 16 + partners // 2 % 16) * 16 + partners // 32 % 8 * 2 + partners % 2

    def lay(x):
        x = x.reshape(Z, own // Z // 2, 2, LINKED).transpose(1, 0, 2, 3).reshape(own, LINKED)
        return jnp.pad(x, ((0, 0), (0, 32 - LINKED)))

    index = jnp.pad(jnp.concatenate([lay(place), lay(types)], axis=1), ((0, 0), (0, 64)))
    offsets = translators.shape[0]
    tr = jnp.pad(translators.reshape(offsets, -1).astype(BF16), ((0, TYPES - offsets), (0, 0)))
    rows = boxes * pairs * excite
    vmem = pl.BlockSpec(memory_space=pltpu.VMEM)
    dma = pltpu.SemaphoreType.DMA
    out = pl.pallas_call(
        kernel,
        out_shape=jax.ShapeDtypeStruct((rows, low), BF16),
        in_specs=[
            pl.BlockSpec(memory_space=pltpu.SMEM),
            vmem,
            pl.BlockSpec(memory_space=pl.ANY),
            vmem,
            vmem,
            vmem,
            vmem,
        ],
        out_specs=vmem,
        scratch_shapes=[
            pltpu.VMEM((Z, low, CHUNK), BF16),
            pltpu.VMEM((Z, 32, CHUNK), BF16),
            pltpu.VMEM((Z, 32, CHUNK), BF16),
            pltpu.VMEM((PLANE, 16, 256), BF16),
            pltpu.VMEM((PLANE, 16, 256), BF16),
            pltpu.VMEM((2, own, 128), jnp.int32),
            pltpu.VMEM((ROWS, TYPES), BF16),
            pltpu.VMEM((BLOCKS, ROWS, 512), BF16),
            pltpu.VMEM((BLOCKS, ROWS, 256), F32),
            pltpu.VMEM((PLANE, 16, 256), BF16),
            pltpu.VMEM((PLANE, 16, 256), BF16),
            pltpu.VMEM((256, CHUNK), BF16),
            pltpu.VMEM((Z, 32, CHUNK), BF16),
            pltpu.VMEM((Z, 32, CHUNK), BF16),
            pltpu.VMEM((rows, CHUNK), BF16),
            pltpu.VMEM((rows, low), F32),
            dma((Z,)), dma((Z,)), dma((Z,)), dma((PLANE,)), dma((PLANE,)), dma, dma,
            dma((PLANE,)), dma((PLANE,)), dma((Z,)), dma((Z,)),
        ],
        compiler_params=pltpu.CompilerParams(
            collective_id=0, has_side_effects=True, vmem_limit_bytes=60 * 1024 * 1024
        ),
    )(
        octant,
        leaf_patterns.reshape(rows, low),
        interp,
        jnp.cos(shift_angle),
        jnp.sin(shift_angle),
        index,
        tr,
    )
    return out.reshape(boxes, pairs, excite, low)


def solution(mesh):
    placed = (
        P(("box", "dir"), None, None, None),
        P(("box", "dir")),
        P(),
        P(),
        P("box", None),
        P("box", None),
        P(None, None, "dir"),
    )
    return jax.shard_map(
        local,
        mesh=mesh,
        in_specs=placed,
        out_specs=P(("box", "dir"), None, None, None),
        check_vma=False,
    )
```

```python
import jax
import jax.numpy as jnp
from jax import lax
from jax.experimental import pallas as pl
from jax.experimental.pallas import tpu as pltpu
from jax.sharding import PartitionSpec as P

MESH = pl.DeviceIdType.MESH
Z = 8
PLANE = 32
WIDTH = 16
CHUNK = PLANE * WIDTH
PB = 64
LINKED = 27
ROWS = PB * LINKED
BLOCKS = Z * 2 * PLANE // PB
TYPES = 384
F32, BF16 = jnp.float32, jnp.bfloat16


def block_transpose(xs):
    block = lax.broadcasted_iota(jnp.int32, xs[0].shape, 1) // 16
    for step in (1, 2, 4):
        low = (block // step) % 2 == 0
        out = list(xs)
        for i in range(8):
            if i & step == 0:
                a, b = xs[i], xs[i + step]
                out[i] = jnp.where(low, a, pltpu.roll(b, 16 * step, 1))
                out[i + step] = jnp.where(low, pltpu.roll(a, 128 - 16 * step, 1), b)
        xs = out
    return xs


def sincos(x):
    n = jnp.floor(x * 0.6366197723675814 + 0.5)
    r = x - n * 1.5703125 - n * 4.837512969970703125e-4 - n * 7.54978995489188216e-8
    w = r * r
    s = r + r * w * (-1.6666654611e-1 + w * (8.3321608736e-3 - w * 1.9515295891e-4))
    c = 1.0 - 0.5 * w + w * w * (4.166664568298827e-2 + w * (-1.388731625493765e-3 + w * 2.443315711809948e-5))
    odd, two = jnp.abs(n) == 1.0, jnp.abs(n) == 2.0
    return jnp.where(odd, n * c, jnp.where(two, -s, s)), jnp.where(odd, -n * s, jnp.where(two, -c, c))


def kernel(
    oct_ref, leaf_ref, interp_ref, angle_ref, partners_ref, types_ref, tr_ref, out_ref,
    cos_ref, sin_ref, flat, idx, trp,
    interp_v, zsend, zrecv, ysend, arecv, idxall, oht, oh, fac, rsend, rrecv, xp, wsend, wrecv, shifted, acc,
    isem, zs, zr, ys, yr, xs_sem, xr_sem, rs, rr, ws, wr,
):
    box = lax.axis_index("box")
    d = lax.axis_index("dir")
    z = d // 16
    yxc = d % 16
    slab = box * 16 + yxc
    spot = yxc * 2 + box

    def plane_of_slab(s):
        return (s // 16, z * 16 + s % 16)

    def plane_of_spot(t):
        return (t % 2, z * 16 + t // 2)

    def order(i):
        half = (i + 1) // 2
        return (z + 4 + half * (1 - 2 * (i % 2))) % 8

    def fetch(i):
        zc = order(i)
        at = pl.multiple_of(zc * CHUNK, CHUNK)
        return pltpu.make_async_copy(interp_ref.at[:, pl.ds(at, CHUNK)], interp_v.at[zc], isem.at[i])

    for i in range(Z):
        fetch(i).start()

    barrier = pltpu.get_barrier_semaphore()

    def greet_z(i, carry):
        pl.semaphore_signal(barrier, inc=1, device_id=(box, (z + i) % 8 * 16 + yxc), device_id_type=MESH)
        return carry

    def greet_plane(i, carry):
        pl.semaphore_signal(barrier, inc=1, device_id=plane_of_slab((slab + i) % PLANE), device_id_type=MESH)
        return carry

    lax.fori_loop(1, Z, greet_z, 0)
    lax.fori_loop(1, PLANE, greet_plane, 0)

    for i in range(Z):
        lanes = slice(i * CHUNK, (i + 1) * CHUNK)
        sin_ref[:, lanes], cos_ref[:, lanes] = sincos(angle_ref[:, lanes])

    def idx_copy(which, ref):
        return pltpu.make_async_remote_copy(
            src_ref=ref, dst_ref=idxall.at[box, which], send_sem=xs_sem.at[which], recv_sem=xr_sem.at[which],
            device_id=(1 - box, d), device_id_type=MESH,
        )

    def z_copy(src, dst, ssem, rsem, zc):
        return pltpu.make_async_remote_copy(
            src_ref=src.at[zc], dst_ref=dst.at[z], send_sem=ssem.at[zc], recv_sem=rsem.at[z],
            device_id=(box, zc * 16 + yxc), device_id_type=MESH,
        )

    def z_arrival(src, dst, ssem, rsem, zc):
        return pltpu.make_async_remote_copy(
            src_ref=src.at[zc], dst_ref=dst.at[zc], send_sem=ssem.at[zc], recv_sem=rsem.at[zc],
            device_id=(box, zc * 16 + yxc), device_id_type=MESH,
        )

    def phases(child, zc):
        o = oct_ref[child]
        at = pl.ds(pl.multiple_of(zc * CHUNK, CHUNK), CHUNK)
        return cos_ref[pl.ds(o, 1), at], sin_ref[pl.ds(o, 1), at]

    def lift(i, carry):
        zc = order(i)
        raise_plane(i, zc)

        @pl.when(i < Z - 1)
        def _():
            z_copy(zsend, zrecv, zs, zr, zc).start()

        return carry

    def raise_plane(i, zc):
        fetch(i).wait()
        up = jnp.dot(leaf_ref[...], interp_v[zc], preferred_element_type=F32)
        parts = []
        for parent in range(2):
            real = imag = None
            for k in range(8):
                child = parent * 8 + k
                cs, sn = phases(child, zc)
                ur, ui = up[child * 16 : child * 16 + 8], up[child * 16 + 8 : child * 16 + 16]
                a, b = ur * cs - ui * sn, ur * sn + ui * cs
                real, imag = (a, b) if real is None else (real + a, imag + b)
            parts += [real, imag]
        zsend[zc] = jnp.concatenate(parts, axis=0).astype(BF16)

    first = order(0)
    raise_plane(0, first)
    pl.semaphore_wait(barrier, Z - 1 + PLANE - 1)
    z_copy(zsend, zrecv, zs, zr, first).start()
    idx_copy(0, partners_ref).start()
    idx_copy(1, types_ref).start()
    lax.fori_loop(1, Z, lift, 0)
    zrecv[z] = zsend[z]

    spread = (
        lax.broadcasted_iota(jnp.int32, (64, 256), 0)
        == lax.broadcasted_iota(jnp.int32, (64, 256), 1) // 128 * 32
        + box * WIDTH
        + lax.broadcasted_iota(jnp.int32, (64, 256), 1) % WIDTH
    )
    trp[...] = jnp.zeros_like(trp)
    trp[:, 0 : tr_ref.shape[1]] = tr_ref[...]
    table = jnp.dot(
        trp[...].T.astype(BF16), spread.astype(F32).astype(BF16), preferred_element_type=F32
    ).astype(BF16)
    idxall[box, 0] = partners_ref[...]
    idxall[box, 1] = types_ref[...]
    idx_copy(0, partners_ref).wait()
    idx_copy(1, types_ref).wait()

    p0 = lax.broadcasted_iota(jnp.int32, (256, 256), 0)
    p1 = lax.broadcasted_iota(jnp.int32, (256, 256), 1)
    place = (p1 == p0 // 2 % 8 * 32 + p0 // 16 * 2 + p0 % 2).astype(F32).astype(BF16)
    nt = (((1,), (1,)), ((), ()))
    flat[...] = jnp.zeros_like(flat)
    for group in range(2):
        p, t = idxall[group, 0], idxall[group, 1]
        high = (p // 256 * 16 + p // 2 % 16) * 16
        flat[0, 0:LINKED] = high.astype(F32)
        flat[0, 32 : 32 + LINKED] = (t // 16 * 16).astype(F32)
        flat[1, 0:LINKED] = (p // 32 % 8 * 2 + p % 2).astype(F32)
        flat[1, 32 : 32 + LINKED] = (t % 16).astype(F32)
        index = lax.dot_general(place, flat[0].astype(BF16), nt, preferred_element_type=F32)
        index += lax.dot_general(place, flat[1].astype(BF16), nt, preferred_element_type=F32)
        idx[group] = index

    def indices(pb):
        half = BLOCKS // 2
        return idx[pb // half, pl.ds(pl.multiple_of(pb % half * PB, PB), PB), :]

    def hot(index, at, lanes):
        wide = lax.broadcasted_iota(jnp.int32, (PB, lanes), 1).astype(F32)
        return (wide == index[:, at : at + 1]).astype(F32).astype(BF16)

    def factors(pb, carry):
        index = indices(pb)
        for k in range(LINKED):
            oht[k * PB : (k + 1) * PB, :] = hot(index, 32 + k, TYPES)
        fac[pb] = jnp.dot(oht[...], table, preferred_element_type=F32)
        return carry

    lax.fori_loop(0, BLOCKS, factors, 0)

    def z_wait(i, carry):
        zc = (z + i) % 8
        z_arrival(zsend, zrecv, zs, zr, zc).wait_recv()
        return carry

    lax.fori_loop(1, Z, z_wait, 0)

    r0 = lax.broadcasted_iota(jnp.int32, (256, 256), 0)
    r1 = lax.broadcasted_iota(jnp.int32, (256, 256), 1)
    turn = (r1 == r0 % 16 * 16 + r0 // 16).astype(F32).astype(BF16)
    turned = jnp.dot(turn, zrecv[...].reshape(256, CHUNK), preferred_element_type=F32)
    for pair in range(2):
        for dh in range(4):
            lanes = slice(dh * 128, dh * 128 + 128)
            blocks = [turned[(pair * 8 + j) * 16 : (pair * 8 + j) * 16 + 16, lanes] for j in range(8)]
            for j, y in enumerate(block_transpose(blocks)):
                ysend[dh * 8 + j, :, pair * 128 : pair * 128 + 128] = y.astype(BF16)

    def y_copy(t):
        return pltpu.make_async_remote_copy(
            src_ref=ysend.at[t], dst_ref=arecv.at[slab], send_sem=ys.at[t], recv_sem=yr.at[slab],
            device_id=plane_of_spot(t), device_id_type=MESH,
        )

    def y_arrival(s):
        return pltpu.make_async_remote_copy(
            src_ref=ysend.at[s], dst_ref=arecv.at[s], send_sem=ys.at[s], recv_sem=yr.at[s],
            device_id=plane_of_slab(s), device_id_type=MESH,
        )

    def y_start(i, carry):
        y_copy((spot + i) % PLANE).start()
        return carry

    lax.fori_loop(1, PLANE, y_start, 0)
    arecv[slab] = ysend[spot]

    def sources(pb, carry):
        index = indices(pb)
        for k in range(LINKED):
            oh[pb, k * PB : (k + 1) * PB, :] = hot(index, k, 512)
        return carry

    lax.fori_loop(0, BLOCKS, sources, 0)

    def y_wait(i, carry):
        y_arrival((slab + i) % PLANE).wait_recv()
        return carry

    lax.fori_loop(1, PLANE, y_wait, 0)

    def r_copy(s):
        return pltpu.make_async_remote_copy(
            src_ref=rsend.at[s], dst_ref=rrecv.at[spot], send_sem=rs.at[s], recv_sem=rr.at[spot],
            device_id=plane_of_slab(s), device_id_type=MESH,
        )

    def r_arrival(t):
        return pltpu.make_async_remote_copy(
            src_ref=rsend.at[t], dst_ref=rrecv.at[t], send_sem=rs.at[t], recv_sem=rr.at[t],
            device_id=plane_of_spot(t), device_id_type=MESH,
        )

    def translate(i, carry):
        pb = (slab * 16 // PB + 1 + i) % BLOCKS
        got = jnp.dot(oh[pb], arecv[...].reshape(512, 256), preferred_element_type=F32)
        real = imag = None
        for k in range(LINKED):
            rows = slice(k * PB, (k + 1) * PB)
            fr, fi = fac[pb, rows, 0:128], fac[pb, rows, 128:256]
            sr, si = got[rows, 0:128], got[rows, 128:256]
            a, b = fr * sr - fi * si, fr * si + fi * sr
            real, imag = (a, b) if real is None else (real + a, imag + b)
        each = jnp.concatenate([real, imag], axis=1).astype(BF16)
        for j in range(PB // 16):
            s = pb * (PB // 16) + j
            rsend[s] = each[j * 16 : j * 16 + 16]

            @pl.when(s != slab)
            def _():
                r_copy(s).start()

        return carry

    lax.fori_loop(0, BLOCKS, translate, 0)
    rrecv[spot] = rsend[slab]

    def r_wait(i, carry):
        r_arrival((spot + i) % PLANE).wait_recv()
        return carry

    lax.fori_loop(1, PLANE, r_wait, 0)

    for pair in range(2):
        for dh in range(4):
            lanes = slice(dh * 128, dh * 128 + 128)
            blocks = [rrecv[dh * 8 + j, :, pair * 128 : pair * 128 + 128].astype(F32) for j in range(8)]
            for j, y in enumerate(block_transpose(blocks)):
                xp[(pair * 8 + j) * 16 : (pair * 8 + j) * 16 + 16, lanes] = y.astype(BF16)
    wsend[...] = jnp.dot(turn, xp[...], preferred_element_type=F32).astype(BF16).reshape(Z, 32, CHUNK)

    def w_start(i, carry):
        z_copy(wsend, wrecv, ws, wr, order(i)).start()
        return carry

    lax.fori_loop(0, Z - 1, w_start, 0)
    wrecv[z] = wsend[z]
    acc[...] = jnp.zeros_like(acc)

    def descend(i, carry):
        zc = order(Z - 1 - i)

        @pl.when(i > 0)
        def _():
            z_arrival(wsend, wrecv, ws, wr, zc).wait_recv()

        got = wrecv[zc].astype(F32)
        for parent in range(2):
            re, im = got[parent * 16 : parent * 16 + 8], got[parent * 16 + 8 : parent * 16 + 16]
            for k in range(8):
                child = parent * 8 + k
                cs, sn = phases(child, zc)
                both = jnp.concatenate([re * cs + im * sn, im * cs - re * sn], axis=0)
                shifted[child * 16 : child * 16 + 16, :] = both.astype(BF16)
        acc[...] += lax.dot_general(
            shifted[...], interp_v[zc], (((1,), (1,)), ((), ())), preferred_element_type=F32
        )
        return carry

    lax.fori_loop(0, Z, descend, 0)
    out_ref[...] = (acc[...] * 0.25).astype(BF16)

    def z_sent(i, carry):
        zc = (z + i) % 8
        z_copy(zsend, zrecv, zs, zr, zc).wait_send()
        z_copy(wsend, wrecv, ws, wr, zc).wait_send()
        return carry

    def plane_sent(i, carry):
        y_copy((spot + i) % PLANE).wait_send()
        r_copy((slab + i) % PLANE).wait_send()
        return carry

    lax.fori_loop(1, Z, z_sent, 0)
    lax.fori_loop(1, PLANE, plane_sent, 0)


def local(leaf_patterns, octant, interp, shift_angle, partners, types, translators):
    boxes, pairs, excite, low = leaf_patterns.shape
    high = interp.shape[1]
    linked, own = partners.shape[1], partners.shape[0]
    offsets = translators.shape[0]
    rows = boxes * pairs * excite
    vmem = pl.BlockSpec(memory_space=pltpu.VMEM)
    dma = pltpu.SemaphoreType.DMA
    out = pl.pallas_call(
        kernel,
        out_shape=jax.ShapeDtypeStruct((rows, low), BF16),
        in_specs=[
            pl.BlockSpec(memory_space=pltpu.SMEM),
            vmem,
            pl.BlockSpec(memory_space=pl.ANY),
            vmem,
            vmem,
            vmem,
            vmem,
        ],
        out_specs=vmem,
        scratch_shapes=[
            pltpu.VMEM((8, high), F32),
            pltpu.VMEM((8, high), F32),
            pltpu.VMEM((2, 128, own), F32),
            pltpu.VMEM((2, own, 128), F32),
            pltpu.VMEM((64, TYPES), F32),
            pltpu.VMEM((Z, low, CHUNK), BF16),
            pltpu.VMEM((Z, 32, CHUNK), BF16),
            pltpu.VMEM((Z, 32, CHUNK), BF16),
            pltpu.VMEM((PLANE, 16, 256), BF16),
            pltpu.VMEM((PLANE, 16, 256), BF16),
            pltpu.VMEM((2, 2, linked, own), jnp.int32),
            pltpu.VMEM((ROWS, TYPES), BF16),
            pltpu.VMEM((BLOCKS, ROWS, 512), BF16),
            pltpu.VMEM((BLOCKS, ROWS, 256), F32),
            pltpu.VMEM((PLANE, 16, 256), BF16),
            pltpu.VMEM((PLANE, 16, 256), BF16),
            pltpu.VMEM((256, CHUNK), BF16),
            pltpu.VMEM((Z, 32, CHUNK), BF16),
            pltpu.VMEM((Z, 32, CHUNK), BF16),
            pltpu.VMEM((rows, CHUNK), BF16),
            pltpu.VMEM((rows, low), F32),
            dma((Z,)), dma((Z,)), dma((Z,)), dma((PLANE,)), dma((PLANE,)), dma((2,)), dma((2,)),
            dma((PLANE,)), dma((PLANE,)), dma((Z,)), dma((Z,)),
        ],
        compiler_params=pltpu.CompilerParams(
            collective_id=0, has_side_effects=True, vmem_limit_bytes=58 * 1024 * 1024
        ),
    )(
        octant,
        leaf_patterns.reshape(rows, low),
        interp,
        shift_angle,
        partners.T,
        types.T,
        translators.transpose(1, 2, 0).reshape(-1, offsets),
    )
    return out.reshape(boxes, pairs, excite, low)


def solution(mesh):
    placed = (
        P(("box", "dir"), None, None, None),
        P(("box", "dir")),
        P(),
        P(),
        P("box", None),
        P("box", None),
        P(None, None, "dir"),
    )
    return jax.shard_map(
        local,
        mesh=mesh,
        in_specs=placed,
        out_specs=P(("box", "dir"), None, None, None),
        check_vma=False,
    )
```

```python
import jax
import jax.numpy as jnp
from jax import lax
from jax.experimental import pallas as pl
from jax.experimental.pallas import tpu as pltpu
from jax.sharding import PartitionSpec as P

MESH = pl.DeviceIdType.MESH
Z = 8
PLANE = 32
WIDTH = 16
CHUNK = PLANE * WIDTH
HALF = CHUNK // 2
PB = 64
LINKED = 27
ROWS = PB * LINKED
BLOCKS = Z * 2 * PLANE // PB
TYPES = 384
F32, BF16 = jnp.float32, jnp.bfloat16


def block_transpose(xs):
    block = lax.broadcasted_iota(jnp.int32, xs[0].shape, 1) // 16
    for step in (1, 2, 4):
        low = (block // step) % 2 == 0
        out = list(xs)
        for i in range(8):
            if i & step == 0:
                a, b = xs[i], xs[i + step]
                out[i] = jnp.where(low, a, pltpu.roll(b, 16 * step, 1))
                out[i + step] = jnp.where(low, pltpu.roll(a, 128 - 16 * step, 1), b)
        xs = out
    return xs


def sincos(x):
    n = jnp.floor(x * 0.6366197723675814 + 0.5)
    r = x - n * 1.5703125 - n * 4.837512969970703125e-4 - n * 7.54978995489188216e-8
    w = r * r
    s = r + r * w * (-1.6666654611e-1 + w * (8.3321608736e-3 - w * 1.9515295891e-4))
    c = 1.0 - 0.5 * w + w * w * (4.166664568298827e-2 + w * (-1.388731625493765e-3 + w * 2.443315711809948e-5))
    odd, two = jnp.abs(n) == 1.0, jnp.abs(n) == 2.0
    return jnp.where(odd, n * c, jnp.where(two, -s, s)), jnp.where(odd, -n * s, jnp.where(two, -c, c))


def kernel(
    oct_ref, leaf_hbm, interp_ref, angle_hbm, partners_hbm, types_hbm, tr_hbm, out_ref,
    leaf_ref, angle_ref, partners_ref, types_ref, tr_ref, in_sem,
    cos_ref, sin_ref, flat, idx, trp,
    interp_v, zsend, zrecv, ysend, arecv, idxall, oht, oh, fac, rsend, rrecv, xp, wsend, wrecv, shifted, acc,
    isem, zs, zr, ys, yr, xs_sem, xr_sem, rs, rr, ws, wr,
):
    box = lax.axis_index("box")
    d = lax.axis_index("dir")
    z = d // 16
    yxc = d % 16
    slab = box * 16 + yxc
    spot = yxc * 2 + box

    def plane_of_slab(s):
        return (s // 16, z * 16 + s % 16)

    def plane_of_spot(t):
        return (t % 2, z * 16 + t // 2)

    def order(i):
        half = (i + 1) // 2
        return (z + 4 + half * (1 - 2 * (i % 2))) % 8

    def half(j):
        return (yxc // 8 + 1 + j) % 2

    def fetch(n):
        h, zc = half(n // Z), order(n % Z)
        at = pl.multiple_of(zc * CHUNK + h * HALF, HALF)
        return pltpu.make_async_copy(interp_ref.at[:, pl.ds(at, HALF)], interp_v.at[zc, h], isem.at[n])

    angle_in = pltpu.make_async_copy(angle_hbm, angle_ref, in_sem.at[0])
    leaf_in = pltpu.make_async_copy(leaf_hbm, leaf_ref, in_sem.at[1])
    partners_in = pltpu.make_async_copy(partners_hbm, partners_ref, in_sem.at[2])
    types_in = pltpu.make_async_copy(types_hbm, types_ref, in_sem.at[3])
    tr_in = pltpu.make_async_copy(tr_hbm, tr_ref, in_sem.at[4])
    angle_in.start()
    leaf_in.start()
    fetch(0).start()
    partners_in.start()
    types_in.start()
    for i in range(1, 2 * Z):
        fetch(i).start()
    tr_in.start()

    barrier = pltpu.get_barrier_semaphore()

    def greet_z(i, carry):
        pl.semaphore_signal(barrier, inc=1, device_id=(box, (z + i) % 8 * 16 + yxc), device_id_type=MESH)
        return carry

    def greet_plane(i, carry):
        pl.semaphore_signal(barrier, inc=1, device_id=plane_of_slab((slab + i) % PLANE), device_id_type=MESH)
        return carry

    lax.fori_loop(1, Z, greet_z, 0)
    lax.fori_loop(1, PLANE, greet_plane, 0)

    angle_in.wait()
    for i in range(Z):
        lanes = slice(i * CHUNK, (i + 1) * CHUNK)
        sin_ref[:, lanes], cos_ref[:, lanes] = sincos(angle_ref[:, lanes])

    def idx_copy(which, ref):
        return pltpu.make_async_remote_copy(
            src_ref=ref, dst_ref=idxall.at[box, which], send_sem=xs_sem.at[which], recv_sem=xr_sem.at[which],
            device_id=(1 - box, d), device_id_type=MESH,
        )

    def z_copy(src, dst, ssem, rsem, h, zc):
        return pltpu.make_async_remote_copy(
            src_ref=src.at[h, zc], dst_ref=dst.at[h, z], send_sem=ssem.at[h, zc], recv_sem=rsem.at[h, z],
            device_id=(box, zc * 16 + yxc), device_id_type=MESH,
        )

    def z_arrival(src, dst, ssem, rsem, h, zc):
        return pltpu.make_async_remote_copy(
            src_ref=src.at[h, zc], dst_ref=dst.at[h, zc], send_sem=ssem.at[h, zc], recv_sem=rsem.at[h, zc],
            device_id=(box, zc * 16 + yxc), device_id_type=MESH,
        )

    def phases(child, h, zc):
        o = oct_ref[child]
        at = pl.ds(pl.multiple_of(zc * CHUNK + h * HALF, HALF), HALF)
        return cos_ref[pl.ds(o, 1), at], sin_ref[pl.ds(o, 1), at]

    def lift(n, carry):
        h, zc = half(n // Z), order(n % Z)
        raise_plane(n, h, zc)

        @pl.when(n % Z < Z - 1)
        def _():
            z_copy(zsend, zrecv, zs, zr, h, zc).start()

        return carry

    def raise_plane(n, h, zc):
        fetch(n).wait()
        up = jnp.dot(leaf_ref[...], interp_v[zc, h], preferred_element_type=F32)
        parts = []
        for parent in range(2):
            real = imag = None
            for k in range(8):
                child = parent * 8 + k
                cs, sn = phases(child, h, zc)
                ur, ui = up[child * 16 : child * 16 + 8], up[child * 16 + 8 : child * 16 + 16]
                a, b = ur * cs - ui * sn, ur * sn + ui * cs
                real, imag = (a, b) if real is None else (real + a, imag + b)
            parts += [real, imag]
        zsend[h, zc] = jnp.concatenate(parts, axis=0).astype(BF16)

    leaf_in.wait()
    raise_plane(0, half(0), order(0))
    pl.semaphore_wait(barrier, Z - 1 + PLANE - 1)
    z_copy(zsend, zrecv, zs, zr, half(0), order(0)).start()
    partners_in.wait()
    types_in.wait()
    idx_copy(0, partners_ref).start()
    idx_copy(1, types_ref).start()
    lax.fori_loop(1, 2 * Z, lift, 0)
    for h in range(2):
        zrecv[h, z] = zsend[h, z]

    spread = (
        lax.broadcasted_iota(jnp.int32, (64, 256), 0)
        == lax.broadcasted_iota(jnp.int32, (64, 256), 1) // 128 * 32
        + box * WIDTH
        + lax.broadcasted_iota(jnp.int32, (64, 256), 1) % WIDTH
    )
    tr_in.wait()
    trp[...] = jnp.zeros_like(trp)
    trp[:, 0 : tr_ref.shape[1]] = tr_ref[...]
    table = jnp.dot(
        trp[...].T.astype(BF16), spread.astype(F32).astype(BF16), preferred_element_type=F32
    ).astype(BF16)
    idxall[box, 0] = partners_ref[...]
    idxall[box, 1] = types_ref[...]
    idx_copy(0, partners_ref).wait()
    idx_copy(1, types_ref).wait()

    p0 = lax.broadcasted_iota(jnp.int32, (256, 256), 0)
    p1 = lax.broadcasted_iota(jnp.int32, (256, 256), 1)
    place = (p1 == p0 // 2 % 8 * 32 + p0 // 16 * 2 + p0 % 2).astype(F32).astype(BF16)
    nt = (((1,), (1,)), ((), ()))
    flat[...] = jnp.zeros_like(flat)
    for group in range(2):
        p, t = idxall[group, 0], idxall[group, 1]
        high = (p // 256 * 16 + p // 2 % 16) * 16
        flat[0, 0:LINKED] = high.astype(F32)
        flat[0, 32 : 32 + LINKED] = (t // 16 * 16).astype(F32)
        flat[1, 0:LINKED] = (p // 32 % 8 * 2 + p % 2).astype(F32)
        flat[1, 32 : 32 + LINKED] = (t % 16).astype(F32)
        index = lax.dot_general(place, flat[0].astype(BF16), nt, preferred_element_type=F32)
        index += lax.dot_general(place, flat[1].astype(BF16), nt, preferred_element_type=F32)
        idx[group] = index

    def indices(pb):
        half = BLOCKS // 2
        return idx[pb // half, pl.ds(pl.multiple_of(pb % half * PB, PB), PB), :]

    def hot(index, at, lanes):
        wide = lax.broadcasted_iota(jnp.int32, (PB, lanes), 1).astype(F32)
        return (wide == index[:, at : at + 1]).astype(F32).astype(BF16)

    def factors(pb, carry):
        index = indices(pb)
        for k in range(LINKED):
            oht[k * PB : (k + 1) * PB, :] = hot(index, 32 + k, TYPES)
        fac[pb] = jnp.dot(oht[...], table, preferred_element_type=F32)
        return carry

    def z_wait(h):
        def wait(i, carry):
            z_arrival(zsend, zrecv, zs, zr, h, (z + i) % 8).wait_recv()
            return carry

        lax.fori_loop(1, Z, wait, 0)

    r0 = lax.broadcasted_iota(jnp.int32, (256, 256), 0)
    r1 = lax.broadcasted_iota(jnp.int32, (256, 256), 1)
    turn = (r1 == r0 % 16 * 16 + r0 // 16).astype(F32).astype(BF16)

    def regroup(h):
        turned = jnp.dot(turn, zrecv[h].reshape(256, HALF), preferred_element_type=F32)
        for pair in range(2):
            for dh in range(2):
                lanes = slice(dh * 128, dh * 128 + 128)
                blocks = [turned[(pair * 8 + j) * 16 : (pair * 8 + j) * 16 + 16, lanes] for j in range(8)]
                for j, y in enumerate(block_transpose(blocks)):
                    ysend[h * 16 + dh * 8 + j, :, pair * 128 : pair * 128 + 128] = y.astype(BF16)

    def y_copy(t):
        return pltpu.make_async_remote_copy(
            src_ref=ysend.at[t], dst_ref=arecv.at[slab], send_sem=ys.at[t], recv_sem=yr.at[slab],
            device_id=plane_of_spot(t), device_id_type=MESH,
        )

    def y_arrival(s):
        return pltpu.make_async_remote_copy(
            src_ref=ysend.at[s], dst_ref=arecv.at[s], send_sem=ys.at[s], recv_sem=yr.at[s],
            device_id=plane_of_slab(s), device_id_type=MESH,
        )

    def y_start(h):
        def start(i, carry):
            y_copy(h * 16 + (spot + i) % 16).start()
            return carry

        return start

    lax.fori_loop(0, 1, factors, 0)
    z_wait(half(0))
    regroup(half(0))
    lax.fori_loop(0, 16, y_start(half(0)), 0)
    lax.fori_loop(1, 5, factors, 0)
    z_wait(half(1))
    regroup(half(1))
    lax.fori_loop(1, 16, y_start(half(1)), 0)
    arecv[slab] = ysend[spot]
    lax.fori_loop(5, BLOCKS, factors, 0)

    def sources(pb, carry):
        index = indices(pb)
        for k in range(LINKED):
            oh[pb, k * PB : (k + 1) * PB, :] = hot(index, k, 512)
        return carry

    lax.fori_loop(0, BLOCKS, sources, 0)

    def y_wait(i, carry):
        y_arrival((slab + i) % PLANE).wait_recv()
        return carry

    lax.fori_loop(1, PLANE, y_wait, 0)

    def r_copy(s):
        return pltpu.make_async_remote_copy(
            src_ref=rsend.at[s], dst_ref=rrecv.at[spot], send_sem=rs.at[s], recv_sem=rr.at[spot],
            device_id=plane_of_slab(s), device_id_type=MESH,
        )

    def r_arrival(t):
        return pltpu.make_async_remote_copy(
            src_ref=rsend.at[t], dst_ref=rrecv.at[t], send_sem=rs.at[t], recv_sem=rr.at[t],
            device_id=plane_of_spot(t), device_id_type=MESH,
        )

    def translate(i, carry):
        y = yxc // 4
        across = (1 - y // 2) * 2 + (y + i // 2) % 2
        near = y // 2 * 2 + (y + 1 - (i // 2) % 2) % 2
        pb = (box + 1 + i) % 2 * 4 + across + (near - across) * (i // 4)
        got = jnp.dot(oh[pb], arecv[...].reshape(512, 256), preferred_element_type=F32)
        real = imag = None
        for k in range(LINKED):
            rows = slice(k * PB, (k + 1) * PB)
            fr, fi = fac[pb, rows, 0:128], fac[pb, rows, 128:256]
            sr, si = got[rows, 0:128], got[rows, 128:256]
            a, b = fr * sr - fi * si, fr * si + fi * sr
            real, imag = (a, b) if real is None else (real + a, imag + b)
        each = jnp.concatenate([real, imag], axis=1).astype(BF16)
        for j in range(PB // 16):
            s = pb * (PB // 16) + j
            rsend[s] = each[j * 16 : j * 16 + 16]

            @pl.when(s != slab)
            def _():
                r_copy(s).start()

        return carry

    def r_wait(h, first):
        def wait(i, carry):
            r_arrival(h * 16 + (spot + i) % 16).wait_recv()
            return carry

        lax.fori_loop(first, 16, wait, 0)

    def ungroup(h):
        for pair in range(2):
            for dh in range(2):
                lanes = slice(dh * 128, dh * 128 + 128)
                blocks = [
                    rrecv[h * 16 + dh * 8 + j, :, pair * 128 : pair * 128 + 128].astype(F32) for j in range(8)
                ]
                for j, y in enumerate(block_transpose(blocks)):
                    xp[(pair * 8 + j) * 16 : (pair * 8 + j) * 16 + 16, lanes] = y.astype(BF16)
        wsend[h] = jnp.dot(turn, xp[...], preferred_element_type=F32).astype(BF16).reshape(Z, 32, HALF)

    def w_start(h):
        def start(i, carry):
            z_copy(wsend, wrecv, ws, wr, h, order(i)).start()
            return carry

        lax.fori_loop(0, Z - 1, start, 0)

    lax.fori_loop(0, 6, translate, 0)
    r_wait(half(0), 0)
    ungroup(half(0))
    w_start(half(0))
    lax.fori_loop(6, BLOCKS, translate, 0)
    rrecv[spot] = rsend[slab]
    r_wait(half(1), 1)
    ungroup(half(1))
    w_start(half(1))
    for h in range(2):
        wrecv[h, z] = wsend[h, z]
    acc[...] = jnp.zeros_like(acc)

    def descend(n, carry):
        terms = []
        for part in range(2):
            i = n % (Z // 2) * 2 + part
            h, zc = half(n // (Z // 2)), order(Z - 1 - i)

            @pl.when(i > 0)
            def _():
                z_arrival(wsend, wrecv, ws, wr, h, zc).wait_recv()

            got = wrecv[h, zc].astype(F32)
            for parent in range(2):
                re, im = got[parent * 16 : parent * 16 + 8], got[parent * 16 + 8 : parent * 16 + 16]
                for k in range(8):
                    child = parent * 8 + k
                    cs, sn = phases(child, h, zc)
                    both = jnp.concatenate([re * cs + im * sn, im * cs - re * sn], axis=0)
                    shifted[part, child * 16 : child * 16 + 16, :] = both.astype(BF16)
            terms.append(
                lax.dot_general(shifted[part], interp_v[zc, h], nt, preferred_element_type=F32)
            )
        acc[...] += terms[0] + terms[1]
        return carry

    lax.fori_loop(0, Z, descend, 0)
    out_ref[...] = (acc[...] * 0.25).astype(BF16)

    def z_sent(i, carry):
        for h in range(2):
            z_copy(zsend, zrecv, zs, zr, h, (z + i) % 8).wait_send()
            z_copy(wsend, wrecv, ws, wr, h, (z + i) % 8).wait_send()
        return carry

    def plane_sent(i, carry):
        y_copy((spot + i) % PLANE).wait_send()
        r_copy((slab + i) % PLANE).wait_send()
        return carry

    lax.fori_loop(1, Z, z_sent, 0)
    lax.fori_loop(1, PLANE, plane_sent, 0)


def local(leaf_patterns, octant, interp, shift_angle, partners, types, translators):
    boxes, pairs, excite, low = leaf_patterns.shape
    high = interp.shape[1]
    linked, own = partners.shape[1], partners.shape[0]
    offsets = translators.shape[0]
    rows = boxes * pairs * excite
    vmem = pl.BlockSpec(memory_space=pltpu.VMEM)
    dma = pltpu.SemaphoreType.DMA
    out = pl.pallas_call(
        kernel,
        out_shape=jax.ShapeDtypeStruct((rows, low), BF16),
        in_specs=[pl.BlockSpec(memory_space=pltpu.SMEM)] + [pl.BlockSpec(memory_space=pltpu.HBM)] * 6,
        out_specs=vmem,
        scratch_shapes=[
            pltpu.VMEM((rows, low), BF16),
            pltpu.VMEM((8, high), F32),
            pltpu.VMEM((linked, own), jnp.int32),
            pltpu.VMEM((linked, own), jnp.int32),
            pltpu.VMEM((64, offsets), F32),
            dma((5,)),
            pltpu.VMEM((8, high), F32),
            pltpu.VMEM((8, high), F32),
            pltpu.VMEM((2, 128, own), F32),
            pltpu.VMEM((2, own, 128), F32),
            pltpu.VMEM((64, TYPES), F32),
            pltpu.VMEM((Z, 2, low, HALF), BF16),
            pltpu.VMEM((2, Z, 32, HALF), BF16),
            pltpu.VMEM((2, Z, 32, HALF), BF16),
            pltpu.VMEM((PLANE, 16, 256), BF16),
            pltpu.VMEM((PLANE, 16, 256), BF16),
            pltpu.VMEM((2, 2, linked, own), jnp.int32),
            pltpu.VMEM((ROWS, TYPES), BF16),
            pltpu.VMEM((BLOCKS, ROWS, 512), BF16),
            pltpu.VMEM((BLOCKS, ROWS, 256), F32),
            pltpu.VMEM((PLANE, 16, 256), BF16),
            pltpu.VMEM((PLANE, 16, 256), BF16),
            pltpu.VMEM((256, HALF), BF16),
            pltpu.VMEM((2, Z, 32, HALF), BF16),
            pltpu.VMEM((2, Z, 32, HALF), BF16),
            pltpu.VMEM((2, rows, HALF), BF16),
            pltpu.VMEM((rows, low), F32),
            dma((2 * Z,)), dma((2, Z)), dma((2, Z)), dma((PLANE,)), dma((PLANE,)), dma((2,)), dma((2,)),
            dma((PLANE,)), dma((PLANE,)), dma((2, Z)), dma((2, Z)),
        ],
        compiler_params=pltpu.CompilerParams(
            collective_id=0, has_side_effects=True, vmem_limit_bytes=58 * 1024 * 1024
        ),
    )(
        octant,
        leaf_patterns.reshape(rows, low),
        interp,
        shift_angle,
        partners.T,
        types.T,
        translators.transpose(1, 2, 0).reshape(-1, offsets),
    )
    return out.reshape(boxes, pairs, excite, low)


def solution(mesh):
    placed = (
        P(("box", "dir"), None, None, None),
        P(("box", "dir")),
        P(),
        P(),
        P("box", None),
        P("box", None),
        P(None, None, "dir"),
    )
    return jax.shard_map(
        local,
        mesh=mesh,
        in_specs=placed,
        out_specs=P(("box", "dir"), None, None, None),
        check_vma=False,
    )
```

```python
import jax
import jax.numpy as jnp
from jax import lax
from jax.experimental import pallas as pl
from jax.experimental.pallas import tpu as pltpu
from jax.sharding import PartitionSpec as P

MESH = pl.DeviceIdType.MESH
Z = 8
PLANE = 32
WIDTH = 16
CHUNK = PLANE * WIDTH
HALF = CHUNK // 2
PB = 64
LINKED = 27
ROWS = PB * LINKED
BLOCKS = Z * 2 * PLANE // PB
TYPES = 384
F32, BF16 = jnp.float32, jnp.bfloat16


def block_transpose(xs):
    block = lax.broadcasted_iota(jnp.int32, xs[0].shape, 1) // 16
    for step in (1, 2, 4):
        low = (block // step) % 2 == 0
        out = list(xs)
        for i in range(8):
            if i & step == 0:
                a, b = xs[i], xs[i + step]
                out[i] = jnp.where(low, a, pltpu.roll(b, 16 * step, 1))
                out[i + step] = jnp.where(low, pltpu.roll(a, 128 - 16 * step, 1), b)
        xs = out
    return xs


def sincos(x):
    n = jnp.floor(x * 0.6366197723675814 + 0.5)
    r = x - n * 1.5703125 - n * 4.837512969970703125e-4 - n * 7.54978995489188216e-8
    w = r * r
    s = r + r * w * (-1.6666654611e-1 + w * (8.3321608736e-3 - w * 1.9515295891e-4))
    c = 1.0 - 0.5 * w + w * w * (4.166664568298827e-2 + w * (-1.388731625493765e-3 + w * 2.443315711809948e-5))
    odd, two = jnp.abs(n) == 1.0, jnp.abs(n) == 2.0
    return jnp.where(odd, n * c, jnp.where(two, -s, s)), jnp.where(odd, -n * s, jnp.where(two, -c, c))


def kernel(
    oct_ref, leaf_hbm, interp_ref, angle_hbm, partners_hbm, types_hbm, tr_hbm, out_ref,
    leaf_ref, angle_ref, partners_ref, types_ref, tr_ref, in_sem,
    cos_ref, sin_ref, flat, idx, trp,
    interp_v, zsend, zrecv, ysend, arecv, idxall, oht, oh, fac, rsend, rrecv, xp, wsend, wrecv, shifted, acc,
    isem, zs, zr, ys, yr, xs_sem, xr_sem, rs, rr, ws, wr,
):
    box = lax.axis_index("box")
    d = lax.axis_index("dir")
    z = d // 16
    yxc = d % 16
    slab = box * 16 + yxc
    spot = yxc * 2 + box

    def wrap(x, n):
        return jnp.where(x >= n, x - n, x)

    def order(i):
        return lax.rem(z + 4 + lax.div(i + 1, 2) * (1 - 2 * lax.rem(i, 2)), 8)

    def half(j):
        return lax.rem(yxc // 8 + 1 + j, 2)

    def fetch(n):
        h, zc = half(lax.div(n, Z)), order(lax.rem(n, Z))
        at = pl.multiple_of(zc * CHUNK + h * HALF, HALF)
        return pltpu.make_async_copy(interp_ref.at[:, pl.ds(at, HALF)], interp_v.at[zc, h], isem.at[n])

    angle_in = pltpu.make_async_copy(angle_hbm, angle_ref, in_sem.at[0])
    leaf_in = pltpu.make_async_copy(leaf_hbm, leaf_ref, in_sem.at[1])
    partners_in = pltpu.make_async_copy(partners_hbm, partners_ref, in_sem.at[2])
    types_in = pltpu.make_async_copy(types_hbm, types_ref, in_sem.at[3])
    tr_in = pltpu.make_async_copy(tr_hbm, tr_ref, in_sem.at[4])
    angle_in.start()
    leaf_in.start()
    fetch(0).start()
    partners_in.start()
    types_in.start()
    for i in range(1, 2 * Z):
        fetch(i).start()
    tr_in.start()

    barrier = pltpu.get_barrier_semaphore()

    def greet(device):
        pl.semaphore_signal(barrier, inc=1, device_id=device, device_id_type=MESH)

    def greet_z(i, carry):
        greet((box, wrap(z + i, Z) * 16 + yxc))
        return carry

    def greet_plane(i, carry):
        for group in range(2):
            greet((group, z * 16 + wrap(yxc + i, 16)))
        return carry

    lax.fori_loop(1, Z, greet_z, 0)
    greet((1 - box, d))
    lax.fori_loop(1, 16, greet_plane, 0)

    def many(src, dst, ssem, rsem):
        return pltpu.make_async_remote_copy(
            src_ref=src, dst_ref=dst, send_sem=ssem, recv_sem=rsem, device_id=(1 - box, d), device_id_type=MESH
        )

    angle_in.wait()
    for i in range(Z):
        lanes = slice(i * CHUNK, (i + 1) * CHUNK)
        sin_ref[:, lanes], cos_ref[:, lanes] = sincos(angle_ref[:, lanes])

    def idx_copy(which, ref):
        return pltpu.make_async_remote_copy(
            src_ref=ref, dst_ref=idxall.at[box, which], send_sem=xs_sem.at[which], recv_sem=xr_sem.at[which],
            device_id=(1 - box, d), device_id_type=MESH,
        )

    def z_copy(src, dst, ssem, rsem, h, zc):
        return pltpu.make_async_remote_copy(
            src_ref=src.at[h, zc], dst_ref=dst.at[h, z], send_sem=ssem.at[h], recv_sem=rsem,
            device_id=(box, zc * 16 + yxc), device_id_type=MESH,
        )

    def phases(child, h, zc):
        o = oct_ref[child]
        at = pl.ds(pl.multiple_of(zc * CHUNK + h * HALF, HALF), HALF)
        return cos_ref[pl.ds(o, 1), at], sin_ref[pl.ds(o, 1), at]

    def lift(n, carry):
        h, zc = half(lax.div(n, Z)), order(lax.rem(n, Z))
        raise_plane(n, h, zc)

        @pl.when(lax.rem(n, Z) < Z - 1)
        def _():
            z_copy(zsend, zrecv, zs, zr.at[h], h, zc).start()

        return carry

    def raise_plane(n, h, zc):
        fetch(n).wait()
        up = jnp.dot(leaf_ref[...], interp_v[zc, h], preferred_element_type=F32)
        parts = []
        for parent in range(2):
            real = imag = None
            for k in range(8):
                child = parent * 8 + k
                cs, sn = phases(child, h, zc)
                ur, ui = up[child * 16 : child * 16 + 8], up[child * 16 + 8 : child * 16 + 16]
                a, b = ur * cs - ui * sn, ur * sn + ui * cs
                real, imag = (a, b) if real is None else (real + a, imag + b)
            parts += [real, imag]
        zsend[h, zc] = jnp.concatenate(parts, axis=0).astype(BF16)

    leaf_in.wait()
    raise_plane(0, half(0), order(jnp.int32(0)))
    pl.semaphore_wait(barrier, Z - 1 + PLANE - 1)
    z_copy(zsend, zrecv, zs, zr.at[half(0)], half(0), order(jnp.int32(0))).start()
    partners_in.wait()
    types_in.wait()
    idx_copy(0, partners_ref).start()
    idx_copy(1, types_ref).start()
    lax.fori_loop(1, 2 * Z, lift, 0)
    for h in range(2):
        zrecv[h, z] = zsend[h, z]

    spread = (
        lax.broadcasted_iota(jnp.int32, (64, 256), 0)
        == lax.broadcasted_iota(jnp.int32, (64, 256), 1) // 128 * 32
        + box * WIDTH
        + lax.broadcasted_iota(jnp.int32, (64, 256), 1) % WIDTH
    )
    tr_in.wait()
    trp[...] = jnp.zeros_like(trp)
    trp[:, 0 : tr_ref.shape[1]] = tr_ref[...]
    table = jnp.dot(
        trp[...].T.astype(BF16), spread.astype(F32).astype(BF16), preferred_element_type=F32
    ).astype(BF16)
    idxall[box, 0] = partners_ref[...]
    idxall[box, 1] = types_ref[...]
    idx_copy(0, partners_ref).wait()
    idx_copy(1, types_ref).wait()

    p0 = lax.broadcasted_iota(jnp.int32, (256, 256), 0)
    p1 = lax.broadcasted_iota(jnp.int32, (256, 256), 1)
    place = (p1 == p0 // 2 % 8 * 32 + p0 // 16 * 2 + p0 % 2).astype(F32).astype(BF16)
    nt = (((1,), (1,)), ((), ()))
    flat[...] = jnp.zeros_like(flat)
    for group in range(2):
        p, t = idxall[group, 0], idxall[group, 1]
        high = (p // 256 * 16 + p // 2 % 16) * 16
        flat[0, 0:LINKED] = high.astype(F32)
        flat[0, 32 : 32 + LINKED] = (t // 16 * 16).astype(F32)
        flat[1, 0:LINKED] = (p // 32 % 8 * 2 + p % 2).astype(F32)
        flat[1, 32 : 32 + LINKED] = (t % 16).astype(F32)
        index = lax.dot_general(place, flat[0].astype(BF16), nt, preferred_element_type=F32)
        index += lax.dot_general(place, flat[1].astype(BF16), nt, preferred_element_type=F32)
        idx[group] = index

    def indices(pb):
        half = BLOCKS // 2
        return idx[pb // half, pl.ds(pl.multiple_of(pb % half * PB, PB), PB), :]

    def hot(index, at, lanes):
        wide = lax.broadcasted_iota(jnp.int32, (PB, lanes), 1).astype(F32)
        return (wide == index[:, at : at + 1]).astype(F32).astype(BF16)

    def factors(pb, carry):
        index = indices(pb)
        for k in range(LINKED):
            oht[k * PB : (k + 1) * PB, :] = hot(index, 32 + k, TYPES)
        fac[pb] = jnp.dot(oht[...], table, preferred_element_type=F32)
        return carry

    def z_all(h):
        most = (h, pl.ds(0, Z - 1))
        return many(zsend.at[most], zrecv.at[most], zs.at[h], zr.at[h])

    r0 = lax.broadcasted_iota(jnp.int32, (256, 256), 0)
    r1 = lax.broadcasted_iota(jnp.int32, (256, 256), 1)
    turn = (r1 == r0 % 16 * 16 + r0 // 16).astype(F32).astype(BF16)

    def regroup(h):
        turned = jnp.dot(turn, zrecv[h].reshape(256, HALF), preferred_element_type=F32)
        for pair in range(2):
            for dh in range(2):
                lanes = slice(dh * 128, dh * 128 + 128)
                blocks = [turned[(pair * 8 + j) * 16 : (pair * 8 + j) * 16 + 16, lanes] for j in range(8)]
                for j, y in enumerate(block_transpose(blocks)):
                    ysend[h * 16 + dh * 8 + j, :, pair * 128 : pair * 128 + 128] = y.astype(BF16)

    def y_start(group, place):
        t = place * 2 + group
        pltpu.make_async_remote_copy(
            src_ref=ysend.at[t], dst_ref=arecv.at[slab], send_sem=ys, recv_sem=yr,
            device_id=(group, z * 16 + place), device_id_type=MESH,
        ).start()

    def y_starts(h):
        def start(i, carry):
            for group in range(2):
                y_start(group, h * 8 + wrap(yxc % 8 + i, 8))
            return carry

        return start

    lax.fori_loop(0, 1, factors, 0)
    z_all(half(0)).wait_recv()
    regroup(half(0))
    lax.fori_loop(0, 8, y_starts(half(0)), 0)
    lax.fori_loop(1, 5, factors, 0)
    z_all(half(1)).wait_recv()
    regroup(half(1))
    y_start(1 - box, yxc)
    lax.fori_loop(1, 8, y_starts(half(1)), 0)
    arecv[slab] = ysend[spot]
    lax.fori_loop(5, BLOCKS, factors, 0)

    def sources(pb, carry):
        index = indices(pb)
        for k in range(LINKED):
            oh[pb, k * PB : (k + 1) * PB, :] = hot(index, k, 512)
        return carry

    lax.fori_loop(0, BLOCKS, sources, 0)

    y_all = many(ysend.at[pl.ds(0, PLANE - 1)], arecv.at[pl.ds(0, PLANE - 1)], ys, yr)
    y_all.wait_recv()

    def translate(i, carry):
        y = yxc // 4
        pair = lax.div(i, 2)
        across = (1 - y // 2) * 2 + lax.rem(y + pair, 2)
        near = y // 2 * 2 + lax.rem(y + 3 - pair, 2)
        row = jnp.where(pair < 2, across, near)
        group = lax.rem(box + 1 + i, 2)
        pb = group * 4 + row
        got = jnp.dot(oh[pb], arecv[...].reshape(512, 256), preferred_element_type=F32)
        real = imag = None
        for k in range(LINKED):
            rows = slice(k * PB, (k + 1) * PB)
            fr, fi = fac[pb, rows, 0:128], fac[pb, rows, 128:256]
            sr, si = got[rows, 0:128], got[rows, 128:256]
            a, b = fr * sr - fi * si, fr * si + fi * sr
            real, imag = (a, b) if real is None else (real + a, imag + b)
        each = jnp.concatenate([real, imag], axis=1).astype(BF16)
        for j in range(PB // 16):
            s = pb * (PB // 16) + j
            rsend[s] = each[j * 16 : j * 16 + 16]

            @pl.when(s != slab)
            def _():
                pltpu.make_async_remote_copy(
                    src_ref=rsend.at[s], dst_ref=rrecv.at[spot], send_sem=rs, recv_sem=rr.at[yxc // 8],
                    device_id=(group, z * 16 + row * 4 + j), device_id_type=MESH,
                ).start()

        return carry

    def r_wait(h, count):
        many(rsend.at[pl.ds(0, count)], rrecv.at[pl.ds(0, count)], rs, rr.at[h]).wait_recv()

    def ungroup(h):
        for pair in range(2):
            for dh in range(2):
                lanes = slice(dh * 128, dh * 128 + 128)
                blocks = [
                    rrecv[h * 16 + dh * 8 + j, :, pair * 128 : pair * 128 + 128].astype(F32) for j in range(8)
                ]
                for j, y in enumerate(block_transpose(blocks)):
                    xp[(pair * 8 + j) * 16 : (pair * 8 + j) * 16 + 16, lanes] = y.astype(BF16)
        wsend[h] = jnp.dot(turn, xp[...], preferred_element_type=F32).astype(BF16).reshape(Z, 32, HALF)

    def w_start(h):
        def start(i, carry):
            z_copy(wsend, wrecv, ws, wr.at[h, z], h, order(i)).start()
            return carry

        lax.fori_loop(0, Z - 1, start, 0)

    lax.fori_loop(0, 6, translate, 0)
    r_wait(half(0), PLANE // 2)
    ungroup(half(0))
    w_start(half(0))
    lax.fori_loop(6, BLOCKS, translate, 0)
    rrecv[spot] = rsend[slab]
    r_wait(half(1), PLANE // 2 - 1)
    ungroup(half(1))
    w_start(half(1))
    for h in range(2):
        wrecv[h, z] = wsend[h, z]
    acc[...] = jnp.zeros_like(acc)

    def descend(n, carry):
        terms = []
        for part in range(2):
            i = lax.rem(n, Z // 2) * 2 + part
            h, zc = half(lax.div(n, Z // 2)), order(Z - 1 - i)

            @pl.when(i > 0)
            def _():
                many(wsend.at[h, zc], wrecv.at[h, zc], ws.at[h], wr.at[h, zc]).wait_recv()

            got = wrecv[h, zc].astype(F32)
            for parent in range(2):
                re, im = got[parent * 16 : parent * 16 + 8], got[parent * 16 + 8 : parent * 16 + 16]
                for k in range(8):
                    child = parent * 8 + k
                    cs, sn = phases(child, h, zc)
                    both = jnp.concatenate([re * cs + im * sn, im * cs - re * sn], axis=0)
                    shifted[part, child * 16 : child * 16 + 16, :] = both.astype(BF16)
            terms.append(
                lax.dot_general(shifted[part], interp_v[zc, h], nt, preferred_element_type=F32)
            )
        acc[...] += terms[0] + terms[1]
        return carry

    lax.fori_loop(0, Z, descend, 0)
    out_ref[...] = acc[...].astype(BF16)

    for h in range(2):
        z_all(h).wait_send()
        most = (h, pl.ds(0, Z - 1))
        many(wsend.at[most], wrecv.at[most], ws.at[h], wr.at[h, 0]).wait_send()
    y_all.wait_send()
    r_most = pl.ds(0, PLANE - 1)
    many(rsend.at[r_most], rrecv.at[r_most], rs, rr.at[0]).wait_send()


def local(leaf_patterns, octant, interp, shift_angle, partners, types, translators):
    boxes, pairs, excite, low = leaf_patterns.shape
    high = interp.shape[1]
    linked, own = partners.shape[1], partners.shape[0]
    offsets = translators.shape[0]
    rows = boxes * pairs * excite
    vmem = pl.BlockSpec(memory_space=pltpu.VMEM)
    dma = pltpu.SemaphoreType.DMA
    out = pl.pallas_call(
        kernel,
        out_shape=jax.ShapeDtypeStruct((rows, low), BF16),
        in_specs=[pl.BlockSpec(memory_space=pltpu.SMEM)] + [pl.BlockSpec(memory_space=pltpu.HBM)] * 6,
        out_specs=vmem,
        scratch_shapes=[
            pltpu.VMEM((rows, low), BF16),
            pltpu.VMEM((8, high), F32),
            pltpu.VMEM((linked, own), jnp.int32),
            pltpu.VMEM((linked, own), jnp.int32),
            pltpu.VMEM((64, offsets), F32),
            dma((5,)),
            pltpu.VMEM((8, high), F32),
            pltpu.VMEM((8, high), F32),
            pltpu.VMEM((2, 128, own), F32),
            pltpu.VMEM((2, own, 128), F32),
            pltpu.VMEM((64, TYPES), F32),
            pltpu.VMEM((Z, 2, low, HALF), BF16),
            pltpu.VMEM((2, Z, 32, HALF), BF16),
            pltpu.VMEM((2, Z, 32, HALF), BF16),
            pltpu.VMEM((PLANE, 16, 256), BF16),
            pltpu.VMEM((PLANE, 16, 256), BF16),
            pltpu.VMEM((2, 2, linked, own), jnp.int32),
            pltpu.VMEM((ROWS, TYPES), BF16),
            pltpu.VMEM((BLOCKS, ROWS, 512), BF16),
            pltpu.VMEM((BLOCKS, ROWS, 256), F32),
            pltpu.VMEM((PLANE, 16, 256), BF16),
            pltpu.VMEM((PLANE, 16, 256), BF16),
            pltpu.VMEM((256, HALF), BF16),
            pltpu.VMEM((2, Z, 32, HALF), BF16),
            pltpu.VMEM((2, Z, 32, HALF), BF16),
            pltpu.VMEM((2, rows, HALF), BF16),
            pltpu.VMEM((rows, low), F32),
            dma((2 * Z,)), dma((2,)), dma((2,)), dma, dma, dma((2,)), dma((2,)),
            dma, dma((2,)), dma((2,)), dma((2, Z)),
        ],
        compiler_params=pltpu.CompilerParams(
            collective_id=0, has_side_effects=True, vmem_limit_bytes=58 * 1024 * 1024
        ),
    )(
        octant,
        leaf_patterns.reshape(rows, low),
        interp,
        shift_angle,
        partners.T,
        types.T,
        translators.transpose(1, 2, 0).reshape(-1, offsets),
    )
    return out.reshape(boxes, pairs, excite, low) * jnp.asarray(low / high, BF16)


def solution(mesh):
    placed = (
        P(("box", "dir"), None, None, None),
        P(("box", "dir")),
        P(),
        P(),
        P("box", None),
        P("box", None),
        P(None, None, "dir"),
    )
    return jax.shard_map(
        local,
        mesh=mesh,
        in_specs=placed,
        out_specs=P(("box", "dir"), None, None, None),
        check_vma=False,
    )
```

```python
import jax
import jax.numpy as jnp
from jax import lax
from jax.experimental import pallas as pl
from jax.experimental.pallas import tpu as pltpu
from jax.sharding import PartitionSpec as P

MESH = pl.DeviceIdType.MESH
Z = 8
PLANE = 32
WIDTH = 16
CHUNK = PLANE * WIDTH
HALF = CHUNK // 2
PB = 64
LINKED = 27
ROWS = PB * LINKED
BLOCKS = Z * 2 * PLANE // PB
TYPES = 384
F32, BF16 = jnp.float32, jnp.bfloat16


def block_transpose(xs):
    block = lax.broadcasted_iota(jnp.int32, xs[0].shape, 1) // 16
    for step in (1, 2, 4):
        low = (block // step) % 2 == 0
        out = list(xs)
        for i in range(8):
            if i & step == 0:
                a, b = xs[i], xs[i + step]
                out[i] = jnp.where(low, a, pltpu.roll(b, 16 * step, 1))
                out[i + step] = jnp.where(low, pltpu.roll(a, 128 - 16 * step, 1), b)
        xs = out
    return xs


def sincos(x):
    n = jnp.floor(x * 0.6366197723675814 + 0.5)
    r = x - n * 1.5703125 - n * 4.837512969970703125e-4 - n * 7.54978995489188216e-8
    w = r * r
    s = r + r * w * (-1.6666654611e-1 + w * (8.3321608736e-3 - w * 1.9515295891e-4))
    c = 1.0 - 0.5 * w + w * w * (4.166664568298827e-2 + w * (-1.388731625493765e-3 + w * 2.443315711809948e-5))
    odd, two = jnp.abs(n) == 1.0, jnp.abs(n) == 2.0
    return jnp.where(odd, n * c, jnp.where(two, -s, s)), jnp.where(odd, -n * s, jnp.where(two, -c, c))


def kernel(
    oct_ref, leaf_hbm, interp_ref, angle_hbm, partners_hbm, types_hbm, tr_hbm, out_ref,
    leaf_ref, angle_ref, partners_ref, types_ref, tr_ref, in_sem,
    cos_ref, sin_ref, flat, idx, trp,
    interp_v, zsend, zrecv, ysend, arecv, idxall, oht, oh, fac, rsend, rrecv, xp, wsend, wrecv, shifted, acc,
    isem, zs, zr, ys, yr, xs_sem, xr_sem, rs, rr, ws, wr,
):
    box = lax.axis_index("box")
    d = lax.axis_index("dir")
    z = d // 16
    yxc = d % 16
    slab = box * 16 + yxc
    spot = yxc * 2 + box

    def wrap(x, n):
        return jnp.where(x >= n, x - n, x)

    def order(i):
        return lax.rem(z + 4 + lax.div(i + 1, 2) * (1 - 2 * lax.rem(i, 2)), 8)

    def half(j):
        return lax.rem(yxc // 8 + 1 + j, 2)

    def fetch(n):
        h, zc = half(lax.div(n, Z)), order(lax.rem(n, Z))
        at = pl.multiple_of(zc * CHUNK + h * HALF, HALF)
        return pltpu.make_async_copy(interp_ref.at[:, pl.ds(at, HALF)], interp_v.at[zc, h], isem.at[n])

    angle_in = pltpu.make_async_copy(angle_hbm, angle_ref, in_sem.at[0])
    leaf_in = pltpu.make_async_copy(leaf_hbm, leaf_ref, in_sem.at[1])
    partners_in = pltpu.make_async_copy(partners_hbm, partners_ref, in_sem.at[2])
    types_in = pltpu.make_async_copy(types_hbm, types_ref, in_sem.at[3])
    tr_in = pltpu.make_async_copy(tr_hbm, tr_ref, in_sem.at[4])
    angle_in.start()
    leaf_in.start()
    fetch(0).start()
    partners_in.start()
    types_in.start()
    for i in range(1, 2 * Z):
        fetch(i).start()
    tr_in.start()

    barrier = pltpu.get_barrier_semaphore()

    def greet(device):
        pl.semaphore_signal(barrier, inc=1, device_id=device, device_id_type=MESH)

    def greet_z(i, carry):
        greet((box, wrap(z + i, Z) * 16 + yxc))
        return carry

    def greet_plane(i, carry):
        for group in range(2):
            greet((group, z * 16 + wrap(yxc + i, 16)))
        return carry

    lax.fori_loop(1, Z, greet_z, 0, unroll=True)
    greet((1 - box, d))
    lax.fori_loop(1, 16, greet_plane, 0, unroll=True)

    def many(src, dst, ssem, rsem):
        return pltpu.make_async_remote_copy(
            src_ref=src, dst_ref=dst, send_sem=ssem, recv_sem=rsem, device_id=(1 - box, d), device_id_type=MESH
        )

    angle_in.wait()
    for i in range(Z):
        lanes = slice(i * CHUNK, (i + 1) * CHUNK)
        sin_ref[:, lanes], cos_ref[:, lanes] = sincos(angle_ref[:, lanes])

    def idx_copy(which, ref):
        return pltpu.make_async_remote_copy(
            src_ref=ref, dst_ref=idxall.at[box, which], send_sem=xs_sem.at[which], recv_sem=xr_sem.at[which],
            device_id=(1 - box, d), device_id_type=MESH,
        )

    def z_copy(src, dst, ssem, rsem, h, zc):
        return pltpu.make_async_remote_copy(
            src_ref=src.at[h, zc], dst_ref=dst.at[h, z], send_sem=ssem.at[h], recv_sem=rsem,
            device_id=(box, zc * 16 + yxc), device_id_type=MESH,
        )

    def phases(child, h, zc):
        o = oct_ref[child]
        at = pl.ds(pl.multiple_of(zc * CHUNK + h * HALF, HALF), HALF)
        return cos_ref[pl.ds(o, 1), at], sin_ref[pl.ds(o, 1), at]

    def lift(n, carry):
        h, zc = half(lax.div(n, Z)), order(lax.rem(n, Z))
        raise_plane(n, h, zc)

        @pl.when(lax.rem(n, Z) < Z - 1)
        def _():
            z_copy(zsend, zrecv, zs, zr.at[h], h, zc).start()

        return carry

    def raise_plane(n, h, zc):
        fetch(n).wait()
        up = jnp.dot(leaf_ref[...], interp_v[zc, h], preferred_element_type=F32)
        parts = []
        for parent in range(2):
            real = imag = None
            for k in range(8):
                child = parent * 8 + k
                cs, sn = phases(child, h, zc)
                ur, ui = up[child * 16 : child * 16 + 8], up[child * 16 + 8 : child * 16 + 16]
                a, b = ur * cs - ui * sn, ur * sn + ui * cs
                real, imag = (a, b) if real is None else (real + a, imag + b)
            parts += [real, imag]
        zsend[h, zc] = jnp.concatenate(parts, axis=0).astype(BF16)

    leaf_in.wait()
    raise_plane(0, half(0), order(jnp.int32(0)))
    pl.semaphore_wait(barrier, Z - 1 + PLANE - 1)
    z_copy(zsend, zrecv, zs, zr.at[half(0)], half(0), order(jnp.int32(0))).start()
    partners_in.wait()
    types_in.wait()
    idx_copy(0, partners_ref).start()
    idx_copy(1, types_ref).start()
    lax.fori_loop(1, 2 * Z, lift, 0)
    for h in range(2):
        zrecv[h, z] = zsend[h, z]

    spread = (
        lax.broadcasted_iota(jnp.int32, (64, 256), 0)
        == lax.broadcasted_iota(jnp.int32, (64, 256), 1) // 128 * 32
        + box * WIDTH
        + lax.broadcasted_iota(jnp.int32, (64, 256), 1) % WIDTH
    )
    tr_in.wait()
    trp[...] = jnp.zeros_like(trp)
    trp[:, 0 : tr_ref.shape[1]] = tr_ref[...]
    table = jnp.dot(
        trp[...].T.astype(BF16), spread.astype(F32).astype(BF16), preferred_element_type=F32
    ).astype(BF16)
    idxall[box, 0] = partners_ref[...]
    idxall[box, 1] = types_ref[...]
    idx_copy(0, partners_ref).wait()
    idx_copy(1, types_ref).wait()

    p0 = lax.broadcasted_iota(jnp.int32, (256, 256), 0)
    p1 = lax.broadcasted_iota(jnp.int32, (256, 256), 1)
    place = (p1 == p0 // 2 % 8 * 32 + p0 // 16 * 2 + p0 % 2).astype(F32).astype(BF16)
    nt = (((1,), (1,)), ((), ()))
    flat[...] = jnp.zeros_like(flat)
    for group in range(2):
        p, t = idxall[group, 0], idxall[group, 1]
        high = (p // 256 * 16 + p // 2 % 16) * 16
        flat[0, 0:LINKED] = high.astype(F32)
        flat[0, 32 : 32 + LINKED] = (t // 16 * 16).astype(F32)
        flat[1, 0:LINKED] = (p // 32 % 8 * 2 + p % 2).astype(F32)
        flat[1, 32 : 32 + LINKED] = (t % 16).astype(F32)
        index = lax.dot_general(place, flat[0].astype(BF16), nt, preferred_element_type=F32)
        index += lax.dot_general(place, flat[1].astype(BF16), nt, preferred_element_type=F32)
        idx[group] = index

    def indices(pb):
        half = BLOCKS // 2
        return idx[pb // half, pl.ds(pl.multiple_of(pb % half * PB, PB), PB), :]

    def hot(index, at, lanes):
        wide = lax.broadcasted_iota(jnp.int32, (PB, lanes), 1).astype(F32)
        return (wide == index[:, at : at + 1]).astype(F32).astype(BF16)

    def factors(pb, carry):
        index = indices(pb)
        for k in range(LINKED):
            oht[k * PB : (k + 1) * PB, :] = hot(index, 32 + k, TYPES)
        fac[pb] = jnp.dot(oht[...], table, preferred_element_type=F32)
        return carry

    def z_all(h):
        most = (h, pl.ds(0, Z - 1))
        return many(zsend.at[most], zrecv.at[most], zs.at[h], zr.at[h])

    r0 = lax.broadcasted_iota(jnp.int32, (256, 256), 0)
    r1 = lax.broadcasted_iota(jnp.int32, (256, 256), 1)
    turn = (r1 == r0 % 16 * 16 + r0 // 16).astype(F32).astype(BF16)

    def regroup(h):
        turned = jnp.dot(turn, zrecv[h].reshape(256, HALF), preferred_element_type=F32)
        for pair in range(2):
            for dh in range(2):
                lanes = slice(dh * 128, dh * 128 + 128)
                blocks = [turned[(pair * 8 + j) * 16 : (pair * 8 + j) * 16 + 16, lanes] for j in range(8)]
                for j, y in enumerate(block_transpose(blocks)):
                    ysend[h * 16 + dh * 8 + j, :, pair * 128 : pair * 128 + 128] = y.astype(BF16)

    def y_start(group, place):
        t = place * 2 + group
        pltpu.make_async_remote_copy(
            src_ref=ysend.at[t], dst_ref=arecv.at[slab], send_sem=ys, recv_sem=yr,
            device_id=(group, z * 16 + place), device_id_type=MESH,
        ).start()

    def y_starts(h):
        def start(i, carry):
            for group in range(2):
                y_start(group, h * 8 + wrap(yxc % 8 + i, 8))
            return carry

        return start

    lax.fori_loop(0, 2, factors, 0)
    z_all(half(0)).wait_recv()
    regroup(half(0))
    lax.fori_loop(0, 8, y_starts(half(0)), 0, unroll=True)
    lax.fori_loop(2, 6, factors, 0)
    z_all(half(1)).wait_recv()
    regroup(half(1))
    y_start(1 - box, yxc)
    lax.fori_loop(1, 8, y_starts(half(1)), 0, unroll=True)
    arecv[slab] = ysend[spot]
    lax.fori_loop(6, BLOCKS, factors, 0)

    def sources(pb, carry):
        index = indices(pb)
        for k in range(LINKED):
            oh[pb, k * PB : (k + 1) * PB, :] = hot(index, k, 512)
        return carry

    lax.fori_loop(0, BLOCKS, sources, 0)

    y_all = many(ysend.at[pl.ds(0, PLANE - 1)], arecv.at[pl.ds(0, PLANE - 1)], ys, yr)
    y_all.wait_recv()

    def translate(i, carry):
        y = yxc // 4
        pair = lax.div(i, 2)
        across = (1 - y // 2) * 2 + lax.rem(y + pair, 2)
        near = y // 2 * 2 + lax.rem(y + 3 - pair, 2)
        row = jnp.where(pair < 2, across, near)
        group = lax.rem(box + 1 + i, 2)
        pb = group * 4 + row
        got = jnp.dot(oh[pb], arecv[...].reshape(512, 256), preferred_element_type=F32)
        real = imag = None
        for k in range(LINKED):
            rows = slice(k * PB, (k + 1) * PB)
            fr, fi = fac[pb, rows, 0:128], fac[pb, rows, 128:256]
            sr, si = got[rows, 0:128], got[rows, 128:256]
            a, b = fr * sr - fi * si, fr * si + fi * sr
            real, imag = (a, b) if real is None else (real + a, imag + b)
        each = jnp.concatenate([real, imag], axis=1).astype(BF16)
        for j in range(PB // 16):
            s = pb * (PB // 16) + j
            rsend[s] = each[j * 16 : j * 16 + 16]

            @pl.when(s != slab)
            def _():
                pltpu.make_async_remote_copy(
                    src_ref=rsend.at[s], dst_ref=rrecv.at[spot], send_sem=rs, recv_sem=rr.at[yxc // 8],
                    device_id=(group, z * 16 + row * 4 + j), device_id_type=MESH,
                ).start()

        return carry

    def r_wait(h, count):
        many(rsend.at[pl.ds(0, count)], rrecv.at[pl.ds(0, count)], rs, rr.at[h]).wait_recv()

    def ungroup(h):
        for pair in range(2):
            for dh in range(2):
                lanes = slice(dh * 128, dh * 128 + 128)
                blocks = [
                    rrecv[h * 16 + dh * 8 + j, :, pair * 128 : pair * 128 + 128].astype(F32) for j in range(8)
                ]
                for j, y in enumerate(block_transpose(blocks)):
                    xp[(pair * 8 + j) * 16 : (pair * 8 + j) * 16 + 16, lanes] = y.astype(BF16)
        wsend[h] = jnp.dot(turn, xp[...], preferred_element_type=F32).astype(BF16).reshape(Z, 32, HALF)

    def w_start(h):
        def start(i, carry):
            z_copy(wsend, wrecv, ws, wr.at[h, z], h, order(i)).start()
            return carry

        lax.fori_loop(0, Z - 1, start, 0, unroll=True)

    lax.fori_loop(0, 7, translate, 0)
    r_wait(half(0), PLANE // 2)
    ungroup(half(0))
    w_start(half(0))
    lax.fori_loop(7, BLOCKS, translate, 0)
    rrecv[spot] = rsend[slab]
    r_wait(half(1), PLANE // 2 - 1)
    ungroup(half(1))
    w_start(half(1))
    for h in range(2):
        wrecv[h, z] = wsend[h, z]
    acc[...] = jnp.zeros_like(acc)

    def descend(n, carry):
        terms = []
        for part in range(2):
            i = lax.rem(n, Z // 2) * 2 + part
            h, zc = half(lax.div(n, Z // 2)), order(Z - 1 - i)

            @pl.when(i > 0)
            def _():
                many(wsend.at[h, zc], wrecv.at[h, zc], ws.at[h], wr.at[h, zc]).wait_recv()

            got = wrecv[h, zc].astype(F32)
            for parent in range(2):
                re, im = got[parent * 16 : parent * 16 + 8], got[parent * 16 + 8 : parent * 16 + 16]
                for k in range(8):
                    child = parent * 8 + k
                    cs, sn = phases(child, h, zc)
                    both = jnp.concatenate([re * cs + im * sn, im * cs - re * sn], axis=0)
                    shifted[part, child * 16 : child * 16 + 16, :] = both.astype(BF16)
            terms.append(
                lax.dot_general(shifted[part], interp_v[zc, h], nt, preferred_element_type=F32)
            )
        acc[...] += terms[0] + terms[1]
        return carry

    lax.fori_loop(0, Z, descend, 0)
    out_ref[...] = acc[...].astype(BF16)

    for h in range(2):
        z_all(h).wait_send()
        most = (h, pl.ds(0, Z - 1))
        many(wsend.at[most], wrecv.at[most], ws.at[h], wr.at[h, 0]).wait_send()
    y_all.wait_send()
    r_most = pl.ds(0, PLANE - 1)
    many(rsend.at[r_most], rrecv.at[r_most], rs, rr.at[0]).wait_send()


def local(leaf_patterns, octant, interp, shift_angle, partners, types, translators):
    boxes, pairs, excite, low = leaf_patterns.shape
    high = interp.shape[1]
    linked, own = partners.shape[1], partners.shape[0]
    offsets = translators.shape[0]
    rows = boxes * pairs * excite
    vmem = pl.BlockSpec(memory_space=pltpu.VMEM)
    dma = pltpu.SemaphoreType.DMA
    out = pl.pallas_call(
        kernel,
        out_shape=jax.ShapeDtypeStruct((rows, low), BF16),
        in_specs=[pl.BlockSpec(memory_space=pltpu.SMEM)] + [pl.BlockSpec(memory_space=pltpu.HBM)] * 6,
        out_specs=vmem,
        scratch_shapes=[
            pltpu.VMEM((rows, low), BF16),
            pltpu.VMEM((8, high), F32),
            pltpu.VMEM((linked, own), jnp.int32),
            pltpu.VMEM((linked, own), jnp.int32),
            pltpu.VMEM((64, offsets), F32),
            dma((5,)),
            pltpu.VMEM((8, high), F32),
            pltpu.VMEM((8, high), F32),
            pltpu.VMEM((2, 128, own), F32),
            pltpu.VMEM((2, own, 128), F32),
            pltpu.VMEM((64, TYPES), F32),
            pltpu.VMEM((Z, 2, low, HALF), BF16),
            pltpu.VMEM((2, Z, 32, HALF), BF16),
            pltpu.VMEM((2, Z, 32, HALF), BF16),
            pltpu.VMEM((PLANE, 16, 256), BF16),
            pltpu.VMEM((PLANE, 16, 256), BF16),
            pltpu.VMEM((2, 2, linked, own), jnp.int32),
            pltpu.VMEM((ROWS, TYPES), BF16),
            pltpu.VMEM((BLOCKS, ROWS, 512), BF16),
            pltpu.VMEM((BLOCKS, ROWS, 256), F32),
            pltpu.VMEM((PLANE, 16, 256), BF16),
            pltpu.VMEM((PLANE, 16, 256), BF16),
            pltpu.VMEM((256, HALF), BF16),
            pltpu.VMEM((2, Z, 32, HALF), BF16),
            pltpu.VMEM((2, Z, 32, HALF), BF16),
            pltpu.VMEM((2, rows, HALF), BF16),
            pltpu.VMEM((rows, low), F32),
            dma((2 * Z,)), dma((2,)), dma((2,)), dma, dma, dma((2,)), dma((2,)),
            dma, dma((2,)), dma((2,)), dma((2, Z)),
        ],
        compiler_params=pltpu.CompilerParams(
            collective_id=0, has_side_effects=True, vmem_limit_bytes=58 * 1024 * 1024
        ),
    )(
        octant,
        leaf_patterns.reshape(rows, low),
        interp,
        shift_angle,
        partners.T,
        types.T,
        translators.transpose(1, 2, 0).reshape(-1, offsets),
    )
    return out.reshape(boxes, pairs, excite, low) * jnp.asarray(low / high, BF16)


def solution(mesh):
    placed = (
        P(("box", "dir"), None, None, None),
        P(("box", "dir")),
        P(),
        P(),
        P("box", None),
        P("box", None),
        P(None, None, "dir"),
    )
    return jax.shard_map(
        local,
        mesh=mesh,
        in_specs=placed,
        out_specs=P(("box", "dir"), None, None, None),
        check_vma=False,
    )
```
